32 devices in a mesh: fsdp: 8 (over z, core), sp: 4 (over y, x).
Axes of the slice: x: 2, y: 2, z: 4, core: 2. Of those that a mesh axis runs over, the one named last changes fastest.
Arguments:
- tokens: bfloat16 [8, 1024, 2048], P('fsdp', 'sp'), may hold values from -6 to 6
- attn_gain: bfloat16 [2048], P('fsdp'), may hold values from 0.5 to 1.5
- attn_shift: bfloat16 [2048], P('fsdp'), may hold values from -1.25 to 1.25
- query_weight: bfloat16 [2048, 2048], P('fsdp'), may hold values from -0.125 to 0.125
- key_weight: bfloat16 [2048, 2048], P('fsdp'), may hold values from -0.125 to 0.125
- value_weight: bfloat16 [2048, 4096], P('fsdp'), may hold values from -0.125 to 0.125
- swish_weight: bfloat16 [2048, 4096], P('fsdp'), may hold values from -0.125 to 0.125
- group_gain: bfloat16 [4096], P('fsdp'), may hold values from 0.5 to 1.5
- group_shift: bfloat16 [4096], P('fsdp'), may hold values from -1.75 to 1.75
- out_weight: bfloat16 [4096, 2048], P('fsdp'), may hold values from -0.125 to 0.125
- ffn_gain: bfloat16 [2048], P('fsdp'), may hold values from 0.5 to 1.5
- ffn_shift: bfloat16 [2048], P('fsdp'), may hold values from -1.25 to 1.25
- gating_weight: bfloat16 [2048, 4096], P('fsdp'), may hold values from -0.125 to 0.125
- upward_weight: bfloat16 [2048, 4096], P('fsdp'), may hold values from -0.125 to 0.125
- gating_bias: bfloat16 [4096], P('fsdp'), may hold values from -1.75 to 1.75
- upward_bias: bfloat16 [4096], P('fsdp'), may hold values from -1.75 to 1.75
- downward_weight: bfloat16 [4096, 2048], P('fsdp'), may hold values from -0.125 to 0.125
- downward_bias: bfloat16 [2048], P('fsdp'), may hold values from -1.25 to 1.25
- cotangent: bfloat16 [8, 1024, 2048], P('fsdp', 'sp'), may hold values from -6 to 6
Outputs:
- layer_out: bfloat16 [8, 1024, 2048], P('fsdp', 'sp')
- input_grad: float32 [8, 1024, 2048], P('fsdp', 'sp')
- attn_gain_grad: float32 [2048], P('fsdp')
- attn_shift_grad: float32 [2048], P('fsdp')
- query_grad: float32 [2048, 2048], P('fsdp')
- key_grad: float32 [2048, 2048], P('fsdp')
- value_grad: float32 [2048, 4096], P('fsdp')
- swish_grad: float32 [2048, 4096], P('fsdp')
- group_gain_grad: float32 [4096], P('fsdp')
- group_shift_grad: float32 [4096], P('fsdp')
- out_weight_grad: float32 [4096, 2048], P('fsdp')
- ffn_gain_grad: float32 [2048], P('fsdp')
- ffn_shift_grad: float32 [2048], P('fsdp')
- gating_grad: float32 [2048, 4096], P('fsdp')
- upward_grad: float32 [2048, 4096], P('fsdp')
- gating_bias_grad: float32 [4096], P('fsdp')
- upward_bias_grad: float32 [4096], P('fsdp')
- downward_grad: float32 [4096, 2048], P('fsdp')
- downward_bias_grad: float32 [2048], P('fsdp')
The draws below stay inside these ranges and needn't reach their ends.
All inputs are finite; a program needn't handle non-finite values.
Results may differ from the reference program's by a relative error of at most 0.02.
Values may be sent and summed in bfloat16 or wider, within the bound.
No kernel may reach another device: no remote copies, remote signals or barrier semaphores. Data moves between devices by JAX's collectives and lax.ppermute only.
A program may use at most 512 MiB of HBM per device.

```python
import math
import jax
import jax.numpy as jnp
from jax import lax

D = 2048
HEADS = 8
QK_HEAD = 256
V_HEAD = 512
FF = 4096
LENGTH = 1024
QK = 2048
VW = 4096
SEQS = 8


def levels(stream_key, dims, shards, least, top_value):
    level, own = 1.0, jax.random.fold_in(stream_key, 6)
    for dim, parts in shards:
        heights = jnp.exp(jax.random.uniform(jax.random.fold_in(own, dim), (parts,), jnp.float32, least / len(shards), top_value / len(shards)))
        level = level * jnp.repeat(heights, dims[dim] // parts).reshape([-1 if axis == dim else 1 for axis in range(len(dims))])
    return level


def gaussian(rng, dims, scale, bound, split=(), dtype=jnp.bfloat16):
    drawn = scale * jax.random.normal(rng, dims, jnp.float32)
    if split:
        drawn = drawn * levels(rng, dims, split, -0.22, 0.18)
    return jnp.clip(drawn, -bound, bound).astype(dtype)


def setup_inputs(seed: int = 0) -> dict:
    streams_of = jax.random.split(jax.random.key(seed), 20)
    tokens = gaussian(streams_of[0], (SEQS, LENGTH, D), 1.0, 6.0, ((0, 8), (1, 4)))
    attn_gain = jnp.clip(1.0 + 0.1 * jax.random.normal(streams_of[1], (D,), jnp.float32), 0.5, 1.5).astype(jnp.bfloat16)
    attn_shift = gaussian(streams_of[2], (D,), 0.2, 1.25, ((0, 8),))
    query_weight = gaussian(streams_of[3], (D, QK), D ** -0.5, 0.125, ((0, 8),))
    key_weight = gaussian(streams_of[4], (D, QK), D ** -0.5, 0.125, ((0, 8),))
    value_weight = gaussian(streams_of[5], (D, VW), D ** -0.5, 0.125, ((0, 8),))
    swish_weight = gaussian(streams_of[6], (D, VW), D ** -0.5, 0.125, ((0, 8),))
    group_gain = jnp.clip(1.0 + 0.1 * jax.random.normal(streams_of[7], (VW,), jnp.float32), 0.5, 1.5).astype(jnp.bfloat16)
    group_shift = gaussian(streams_of[8], (VW,), 0.3, 1.75, ((0, 8),))
    out_weight = gaussian(streams_of[9], (VW, D), (VW // 2) ** -0.5, 0.125, ((0, 8),))
    ffn_gain = jnp.clip(1.0 + 0.1 * jax.random.normal(streams_of[10], (D,), jnp.float32), 0.5, 1.5).astype(jnp.bfloat16)
    ffn_shift = gaussian(streams_of[11], (D,), 0.2, 1.25, ((0, 8),))
    gating_weight = gaussian(streams_of[12], (D, FF), D ** -0.5, 0.125, ((0, 8),))
    upward_weight = gaussian(streams_of[13], (D, FF), D ** -0.5, 0.125, ((0, 8),))
    gating_bias = gaussian(streams_of[14], (FF,), 0.3, 1.75, ((0, 8),))
    upward_bias = gaussian(streams_of[15], (FF,), 0.3, 1.75, ((0, 8),))
    downward_weight = gaussian(streams_of[16], (FF, D), (FF // 2) ** -0.5, 0.125, ((0, 8),))
    downward_bias = gaussian(streams_of[17], (D,), 0.2, 1.25, ((0, 8),))
    cotangent = gaussian(streams_of[18], (SEQS, LENGTH, D), 1.0, 6.0, ((0, 8), (1, 4)))
    return {"tokens": tokens, "attn_gain": attn_gain, "attn_shift": attn_shift, "query_weight": query_weight, "key_weight": key_weight, "value_weight": value_weight, "swish_weight": swish_weight, "group_gain": group_gain, "group_shift": group_shift, "out_weight": out_weight, "ffn_gain": ffn_gain, "ffn_shift": ffn_shift, "gating_weight": gating_weight, "upward_weight": upward_weight, "gating_bias": gating_bias, "upward_bias": upward_bias, "downward_weight": downward_weight, "downward_bias": downward_bias, "cotangent": cotangent}


@jax.custom_vjp
def low(v):
    return lax.optimization_barrier(v.astype(jnp.bfloat16)).astype(jnp.float32)

@jax.custom_vjp
def low_back(v):
    return v

def low_keep(v):
    return (low(v), None)

def low_pass(kept, grad):
    return (grad,)

def back_keep(v):
    return (v, None)

def back_low(kept, grad):
    return (low(grad),)
low.defvjp(low_keep, low_pass)
low_back.defvjp(back_keep, back_low)

def matmul(left, right):
    return jnp.dot(left, right, precision=lax.Precision.HIGHEST, preferred_element_type=jnp.float32)

def layer_norm(values, gain, shift):
    middle = lax.optimization_barrier(jnp.mean(values, -1, keepdims=True))
    centred = values - middle
    spread = lax.optimization_barrier(jnp.mean(centred * centred, -1, keepdims=True))
    return centred * lax.rsqrt(spread + 1e-05) * gain + shift

def decay_mask(head_ids):
    rates = jnp.log(1.0 - jnp.exp2(-5.0 - head_ids.astype(jnp.float32)))
    places = jnp.arange(LENGTH)
    distance = places[:, None] - places[None, :]
    steps = jnp.maximum(distance, 0).astype(jnp.float32)
    return jnp.where(distance[None] >= 0, jnp.exp(steps[None] * rates[:, None, None]), 0.0)

def one_head(operands):
    query, keys, values, mask = operands
    scores = low_back(jnp.einsum('gid,gjd->gij', query, keys, precision=lax.Precision.HIGHEST) * QK_HEAD ** (-0.5))
    weights = low(scores * mask)
    return low(low_back(jnp.einsum('gij,gje->gie', weights, values, precision=lax.Precision.HIGHEST)))

def forward(block_tokens, params):
    attn_gain, attn_shift, query_weight, key_weight, value_weight, swish_weight, group_gain, group_shift, out_weight, ffn_gain, ffn_shift, gating_weight, upward_weight, gating_bias, upward_bias, downward_weight, downward_bias = params
    count = block_tokens.shape[0]
    flat = block_tokens.reshape(-1, D)
    first = low(layer_norm(flat, attn_gain, attn_shift))
    query = low(low_back(matmul(first, query_weight)))
    keys = low(low_back(matmul(first, key_weight)))
    values = low(low_back(matmul(first, value_weight)))
    swish_pre = low_back(matmul(first, swish_weight))

    def by_head(array, width):
        return array.reshape(count, LENGTH, HEADS, width).transpose(2, 0, 1, 3)
    masks = decay_mask(jnp.arange(HEADS))
    outputs = lax.map(jax.checkpoint(one_head), (by_head(query, QK_HEAD), by_head(keys, QK_HEAD), by_head(values, V_HEAD), masks))
    retained = outputs.transpose(1, 2, 0, 3).reshape(-1, HEADS, V_HEAD)
    middle = lax.optimization_barrier(jnp.mean(retained, -1, keepdims=True))
    centred = retained - middle
    spread = lax.optimization_barrier(jnp.mean(centred * centred, -1, keepdims=True))
    grouped = (centred * lax.rsqrt(jnp.maximum(spread, 1.0))).reshape(-1, VW) * group_gain + group_shift
    mixed = low(grouped * jax.nn.silu(swish_pre))
    resid = flat + low_back(matmul(mixed, out_weight))
    second = low(layer_norm(resid, ffn_gain, ffn_shift))
    gating = low_back(matmul(second, gating_weight) + gating_bias)
    upward = low_back(matmul(second, upward_weight) + upward_bias)
    hidden = low(jax.nn.silu(gating) * upward)
    result = resid + matmul(hidden, downward_weight) + downward_bias
    return result.reshape(count, LENGTH, D)

def reference(tokens, attn_gain, attn_shift, query_weight, key_weight, value_weight, swish_weight, group_gain, group_shift, out_weight, ffn_gain, ffn_shift, gating_weight, upward_weight, gating_bias, upward_bias, downward_weight, downward_bias, cotangent):
    params = tuple((item.astype(jnp.float32) for item in (attn_gain, attn_shift, query_weight, key_weight, value_weight, swish_weight, group_gain, group_shift, out_weight, ffn_gain, ffn_shift, gating_weight, upward_weight, gating_bias, upward_bias, downward_weight, downward_bias)))
    group = math.gcd(SEQS, max(1, 4096 // LENGTH))
    shaped_tokens = tokens.astype(jnp.float32).reshape(SEQS // group, group, LENGTH, D)
    shaped_cot = cotangent.astype(jnp.float32).reshape(SEQS // group, group, LENGTH, D)

    def step(totals, batch):
        block_tokens, block_cot = batch
        result, pullback = jax.vjp(forward, block_tokens, params)
        token_grad, param_grads = pullback(block_cot)
        totals = jax.tree.map(lambda left, right: left + right, totals, param_grads)
        return (totals, (result.astype(jnp.bfloat16), token_grad))
    zeros = jax.tree.map(jnp.zeros_like, params)
    totals, (outputs, token_grads) = lax.scan(step, zeros, (shaped_tokens, shaped_cot))
    attn_gain_grad, attn_shift_grad, query_grad, key_grad, value_grad, swish_grad, group_gain_grad, group_shift_grad, out_weight_grad, ffn_gain_grad, ffn_shift_grad, gating_grad, upward_grad, gating_bias_grad, upward_bias_grad, downward_grad, downward_bias_grad = totals
    return (outputs.reshape(SEQS, LENGTH, D), token_grads.reshape(SEQS, LENGTH, D), attn_gain_grad, attn_shift_grad, query_grad, key_grad, value_grad, swish_grad, group_gain_grad, group_shift_grad, out_weight_grad, ffn_gain_grad, ffn_shift_grad, gating_grad, upward_grad, gating_bias_grad, upward_bias_grad, downward_grad, downward_bias_grad)
```

```python
import jax
import jax.numpy as jnp
from jax import lax
from jax.sharding import PartitionSpec as P

HEADS = 8
EPSILON = 1e-05
BF16 = jnp.bfloat16
F32 = jnp.float32


def product(left, right):
    return jnp.dot(left, right, preferred_element_type=F32)


def over_rows(left, right):
    return lax.dot_general(left, right, (((0,), (0,)), ((), ())), preferred_element_type=F32)


def over_columns(left, right):
    return lax.dot_general(left, right, (((1,), (1,)), ((), ())), preferred_element_type=F32)


def normalize(values):
    middle = jnp.mean(values, -1, keepdims=True)
    centred = values - middle
    spread = jnp.mean(centred * centred, -1, keepdims=True)
    factor = lax.rsqrt(spread + EPSILON)
    return (centred * factor, factor)


def group_normalize(values):
    middle = jnp.mean(values, -1, keepdims=True)
    centred = values - middle
    spread = jnp.mean(centred * centred, -1, keepdims=True)
    factor = lax.rsqrt(jnp.maximum(spread, 1.0))
    active = jnp.where(spread > 1.0, 1.0, 0.0)
    return (centred * factor, factor, active)


def normalize_back(scaled, normed, factor, active=1.0):
    first_mean = jnp.mean(scaled, -1, keepdims=True)
    second_mean = jnp.mean(scaled * normed, -1, keepdims=True)
    return factor * (scaled - first_mean - active * normed * second_mean)


def silu_slope(values):
    sigma = jax.nn.sigmoid(values)
    return sigma * (1.0 + values * (1.0 - sigma))


def decay_mask(head_ids, length):
    rates = jnp.log(1.0 - jnp.exp2(-5.0 - head_ids.astype(F32)))
    places = jnp.arange(length)
    distance = places[:, None] - places[None, :]
    steps = jnp.maximum(distance, 0).astype(F32)
    return jnp.where(distance[None] >= 0, jnp.exp(steps[None] * rates[:, None, None]), 0.0)


def split_heads(array, heads_here):
    return array.reshape(array.shape[0], heads_here, -1)


def score_block(query_split, key_split):
    factor = query_split.shape[-1] ** (-0.5)
    raw = jnp.einsum("ihd,jhd->hij", query_split, key_split, preferred_element_type=F32)
    return raw * factor


def retain(query, key, value, mask, heads_here):
    query_split = split_heads(query, heads_here)
    key_split = split_heads(key, heads_here)
    value_split = split_heads(value, heads_here)
    weights = (score_block(query_split, key_split) * mask).astype(BF16)
    output = jnp.einsum("hij,jhe->ihe", weights, value_split, preferred_element_type=F32)
    return output.astype(BF16)


def retain_back(query, key, value, grad_split, mask, heads_here):
    query_split = split_heads(query, heads_here)
    key_split = split_heads(key, heads_here)
    value_split = split_heads(value, heads_here)
    factor = query_split.shape[-1] ** (-0.5)
    weights = (score_block(query_split, key_split) * mask).astype(BF16)
    value_back = jnp.einsum("hij,ihe->jhe", weights, grad_split, preferred_element_type=F32)
    weight_back = jnp.einsum("ihe,jhe->hij", grad_split, value_split, preferred_element_type=F32)
    score_back = (weight_back * mask).astype(BF16)
    query_back = jnp.einsum("hij,jhd->ihd", score_back, key_split, preferred_element_type=F32) * factor
    key_back = jnp.einsum("hij,ihd->jhd", score_back, query_split, preferred_element_type=F32) * factor
    length = query.shape[0]
    return (
        query_back.astype(BF16).reshape(length, -1),
        key_back.astype(BF16).reshape(length, -1),
        value_back.astype(BF16).reshape(length, -1),
    )


class Ring:
    def __init__(self, size):
        half = size // 2
        self.size = size
        self.half = half
        self.order = list(range(half)) + list(range(size - 1, half - 1, -1))
        place = [0] * size
        for position, rank in enumerate(self.order):
            place[rank] = position
        self.right = [(self.order[i], self.order[(i + 1) % size]) for i in range(size)]
        self.left = [(self.order[i], self.order[(i - 1) % size]) for i in range(size)]
        self.me = lax.axis_index("sp")
        self.position = jnp.array(place, jnp.int32)[self.me]

    def rank(self, step):
        return jnp.array(self.order, jnp.int32)[lax.rem(self.position + step + self.size, self.size)]

    def to_right(self, block):
        return lax.ppermute(block, "sp", self.right)

    def to_left(self, block):
        return lax.ppermute(block, "sp", self.left)

    def gather(self, block):
        middle = block.shape[0] // 2
        found = [(0, block)]
        from_left, from_right = block, block
        for step in range(1, self.half):
            from_left, from_right = self.to_right(from_left), self.to_left(from_right)
            found += [(-step, from_left), (step, from_right)]
        low = self.to_right(from_left[:middle])
        high = self.to_left(from_right[middle:])
        found.append((self.half, jnp.concatenate([low, high], 0)))
        out = jnp.zeros((self.size,) + block.shape, block.dtype)
        for step, part in found:
            out = lax.dynamic_update_slice(out, part[None], (self.rank(step), 0, 0))
        return out

    def scatter_sum(self, make):
        far = make(self.rank(self.half)).astype(BF16)
        middle = far.shape[0] // 2
        from_left, from_right = self.to_right(far[:middle]), self.to_left(far[middle:])
        for step in range(self.half - 1, 0, -1):
            ahead, behind = make(self.rank(step)), make(self.rank(-step))
            if step == self.half - 1:
                ahead = jnp.concatenate([ahead[:middle] + from_left.astype(F32), ahead[middle:]], 0)
                behind = jnp.concatenate([behind[:middle], behind[middle:] + from_right.astype(F32)], 0)
            else:
                ahead = ahead + from_left.astype(F32)
                behind = behind + from_right.astype(F32)
            from_left, from_right = self.to_right(ahead.astype(BF16)), self.to_left(behind.astype(BF16))
        return make(self.me) + from_left.astype(F32) + from_right.astype(F32)


def butterfly(vector):
    for axis in ("fsdp", "sp"):
        size = lax.axis_size(axis)
        step = 1
        while step < size:
            vector = vector + lax.ppermute(vector, axis, [(i, i ^ step) for i in range(size)])
            step *= 2
    return vector


def spread_pairs(shards, parts):
    per_block = shards // parts
    pairs = []
    for shard in range(shards):
        for piece in range(parts):
            block, inner = divmod(shard, per_block)
            pairs.append((shard * parts + piece, (inner * parts + piece) * parts + block))
    return pairs


def local(
    tokens,
    attn_gain,
    attn_shift,
    query_weight,
    key_weight,
    value_weight,
    swish_weight,
    group_gain,
    group_shift,
    out_weight,
    ffn_gain,
    ffn_shift,
    gating_weight,
    upward_weight,
    gating_bias,
    upward_bias,
    downward_weight,
    downward_bias,
    cotangent,
):
    seq_count, local_len, width = tokens.shape
    assert seq_count == 1
    parts = lax.axis_size("sp")
    shards = lax.axis_size("fsdp")
    me = lax.axis_index("sp")
    ring = Ring(parts)
    heads_here = HEADS // parts
    full_len = local_len * parts
    value_all = value_weight.shape[1]
    hidden_all = gating_weight.shape[1]
    value_width = value_all // parts
    hidden_width = hidden_all // parts
    query_width = query_weight.shape[1] // parts
    chunk = hidden_width // shards

    def columns(weight):
        size = weight.shape[1] // parts
        return lax.dynamic_slice_in_dim(weight, me * size, size, 1)

    def units(weight):
        pieces = [
            lax.dynamic_slice_in_dim(weight, (i * parts + me) * chunk, chunk, weight.ndim - 1)
            for i in range(shards)
        ]
        return jnp.concatenate(pieces, -1)

    def gathered(array):
        return lax.all_gather(array, "fsdp", axis=0, tiled=True)

    qkv_slice = jnp.concatenate([columns(query_weight), columns(key_weight), columns(value_weight)], 1)
    qkv_full = gathered(qkv_slice)
    swish_full = gathered(columns(swish_weight))
    spread = spread_pairs(shards, parts)
    rows = out_weight.shape[0] // parts
    out_piece = lax.ppermute(
        lax.dynamic_slice_in_dim(out_weight, me * rows, rows, 0), ("fsdp", "sp"), spread
    )
    out_full = gathered(out_piece)
    both_full = gathered(jnp.concatenate([units(gating_weight), units(upward_weight)], 1))
    down_full = gathered(lax.dynamic_slice_in_dim(downward_weight, me * rows, rows, 0))

    small = [
        attn_gain, attn_shift, group_gain, group_shift, ffn_gain, ffn_shift,
        gating_bias, upward_bias, downward_bias,
    ]
    sizes = [item.shape[0] for item in small]
    stacked = gathered(jnp.concatenate(small, 0)[None])
    offsets = [sum(sizes[:i]) for i in range(len(sizes))]
    (
        gain_one, shift_one, ggain_all, gshift_all, gain_two, shift_two, gbias_all, ubias_all, dbias,
    ) = (
        stacked[:, start : start + size].reshape(-1).astype(F32)
        for start, size in zip(offsets, sizes)
    )
    ggain = lax.dynamic_slice_in_dim(ggain_all, me * value_width, value_width, 0)
    gshift = lax.dynamic_slice_in_dim(gshift_all, me * value_width, value_width, 0)
    gbias = units(gbias_all)
    ubias = units(ubias_all)

    flat = tokens.reshape(-1, width).astype(F32)
    first_norm, first_factor = normalize(flat)
    first = ring.gather((first_norm * gain_one + shift_one).astype(BF16)).reshape(full_len, width)
    grad_own = cotangent.reshape(-1, width)
    grad_low = ring.gather(grad_own).reshape(full_len, width)
    qkv = product(first, qkv_full).astype(BF16)
    query, key, value = (
        qkv[:, :query_width], qkv[:, query_width : 2 * query_width], qkv[:, 2 * query_width :],
    )
    head_ids = me * heads_here + jnp.arange(heads_here)
    mask = decay_mask(head_ids, full_len)
    retained = retain(query, key, value, mask, heads_here).astype(F32)
    group_norm3, group_factor, group_active = group_normalize(retained)
    group_norm = group_norm3.reshape(full_len, value_width)
    grouped = group_norm * ggain + gshift
    swish_pre = product(first, swish_full)
    swish_gate = jax.nn.silu(swish_pre)
    mixed = (grouped * swish_gate).astype(BF16)

    def rows_of(array, rank):
        return lax.dynamic_slice_in_dim(array, rank * local_len, local_len, 0)

    resid = flat + ring.scatter_sum(lambda rank: product(rows_of(mixed, rank), out_full))
    second_norm, second_factor = normalize(resid)
    second = ring.gather((second_norm * gain_two + shift_two).astype(BF16)).reshape(full_len, width)
    both = product(second, both_full)
    gating = both[:, :hidden_width] + gbias
    upward = both[:, hidden_width:] + ubias
    gate_act = jax.nn.silu(gating)
    hidden = (gate_act * upward).astype(BF16)

    dhidden = over_columns(grad_low, down_full)
    dgating = (dhidden * upward * silu_slope(gating)).astype(BF16)
    dupward = (dhidden * gate_act).astype(BF16)
    dboth = jnp.concatenate([dgating, dupward], 1)
    gbias_term = jnp.sum(dgating.astype(F32), 0)
    ubias_term = jnp.sum(dupward.astype(F32), 0)

    def summed(term):
        return lax.psum_scatter(term.astype(BF16), "fsdp", scatter_dimension=0, tiled=True)

    both_share = summed(over_rows(second, dboth))
    down_share = summed(over_rows(hidden, grad_low))
    dsecond = ring.scatter_sum(lambda rank: over_columns(rows_of(dboth, rank), both_full))
    fgain_term = jnp.sum(dsecond * second_norm, 0)
    fshift_term = jnp.sum(dsecond, 0)
    grad_out = grad_own.astype(F32)
    dbias_term = jnp.sum(grad_out, 0)
    dresid = grad_out + normalize_back(dsecond * gain_two, second_norm, second_factor)
    dres_low = ring.gather(dresid.astype(BF16)).reshape(full_len, width)
    out_share = summed(over_rows(mixed, dres_low))
    dmixed = over_columns(dres_low, out_full)
    dgrouped = dmixed * swish_gate
    dswish = (dmixed * grouped * silu_slope(swish_pre)).astype(BF16)
    swish_share = summed(over_rows(first, dswish))
    ggain_term = jnp.sum(dgrouped * group_norm, 0)
    gshift_term = jnp.sum(dgrouped, 0)
    dnormed = (dgrouped * ggain).reshape(full_len, heads_here, -1)
    dretained = normalize_back(dnormed, group_norm3, group_factor, group_active).astype(BF16)
    dqkv = jnp.concatenate(retain_back(query, key, value, dretained, mask, heads_here), 1)
    qkv_share = summed(over_rows(first, dqkv))
    dfirst = ring.scatter_sum(
        lambda rank: over_columns(rows_of(dqkv, rank), qkv_full)
        + over_columns(rows_of(dswish, rank), swish_full)
    )
    again_term = jnp.sum(dfirst * first_norm, 0)
    ashift_term = jnp.sum(dfirst, 0)
    input_grad = dresid + normalize_back(dfirst * gain_one, first_norm, first_factor)

    result = ring.scatter_sum(lambda rank: product(rows_of(hidden, rank), down_full))
    layer_out = (resid + result + dbias).astype(BF16)

    def by_columns(share):
        return jnp.moveaxis(ring.gather(share), 0, 1)

    qkv_all = by_columns(qkv_share).astype(F32)
    owned = qkv_share.shape[0]
    query_grad = qkv_all[:, :, :query_width].reshape(owned, -1)
    key_grad = qkv_all[:, :, query_width : 2 * query_width].reshape(owned, -1)
    value_grad = qkv_all[:, :, 2 * query_width :].reshape(owned, -1)
    swish_grad = by_columns(swish_share).astype(F32).reshape(owned, -1)
    both_all = ring.gather(both_share).astype(F32)
    both_all = both_all.reshape(parts, owned, 2, shards, chunk).transpose(2, 1, 3, 0, 4)
    both_all = both_all.reshape(2, owned, hidden_all)
    back = [(target, source) for source, target in spread]
    out_share = lax.ppermute(out_share, ("fsdp", "sp"), back)
    out_grad = ring.gather(out_share).astype(F32).reshape(-1, width)
    downward_grad = ring.gather(down_share).astype(F32).reshape(-1, width)

    def placed(term, whole):
        return lax.dynamic_update_slice(jnp.zeros((whole,), F32), term, (me * term.shape[0],))

    def placed_units(term):
        blank = jnp.zeros((shards, parts, chunk), F32)
        return lax.dynamic_update_slice(blank, term.reshape(shards, 1, chunk), (0, me, 0)).reshape(-1)

    terms = [
        again_term, ashift_term, placed(ggain_term, value_all), placed(gshift_term, value_all),
        fgain_term, fshift_term, placed_units(gbias_term), placed_units(ubias_term), dbias_term,
    ]
    totals = butterfly(jnp.concatenate([term.reshape(shards, -1) for term in terms], 1))
    mine = lax.dynamic_slice_in_dim(totals, lax.axis_index("fsdp"), 1, 0)[0]
    (
        again_grad, ashift_grad, ggain_grad, gshift_grad, fgain_grad, fshift_grad,
        gbias_grad, ubias_grad, dbias_grad,
    ) = (mine[start : start + size] for start, size in zip(offsets, sizes))
    return (
        layer_out.reshape(seq_count, local_len, width),
        input_grad.reshape(seq_count, local_len, width),
        again_grad,
        ashift_grad,
        query_grad,
        key_grad,
        value_grad,
        swish_grad,
        ggain_grad,
        gshift_grad,
        out_grad,
        fgain_grad,
        fshift_grad,
        both_all[0],
        both_all[1],
        gbias_grad,
        ubias_grad,
        downward_grad,
        dbias_grad,
    )


def solution(mesh):
    row, vector, cube = P("fsdp", None), P("fsdp"), P("fsdp", "sp", None)
    return jax.shard_map(
        local,
        mesh=mesh,
        in_specs=(
            cube, vector, vector, row, row, row, row, vector, vector, row,
            vector, vector, row, row, vector, vector, row, vector, cube,
        ),
        out_specs=(
            cube, cube, vector, vector, row, row, row, row, vector, vector,
            row, vector, vector, row, row, vector, vector, row, vector,
        ),
        check_vma=False,
    )
```

```python
import functools

import jax
import jax.numpy as jnp
from jax import lax
from jax.experimental import pallas as pl
from jax.experimental.pallas import tpu as pltpu
from jax.sharding import PartitionSpec as P

HEADS = 8
EPSILON = 1e-05
BF16 = jnp.bfloat16
F32 = jnp.float32
COST = pl.CostEstimate(flops=1024, bytes_accessed=1024, transcendentals=0)
UNREAD = pl.BlockSpec(memory_space=pl.ANY)
NT = (((1,), (1,)), ((), ()))
NN = (((1,), (0,)), ((), ()))
TN = (((0,), (0,)), ((), ()))


def dot(left, right, dims):
    return lax.dot_general(left, right, dims, preferred_element_type=F32)


def product(left, right):
    return dot(left, right, NN)


def over_rows(left, right):
    return dot(left, right, TN)


def after(value, *others):
    return lax.optimization_barrier((value,) + others)[0]


def normalize(values):
    middle = jnp.mean(values, -1, keepdims=True)
    centred = values - middle
    spread = jnp.mean(centred * centred, -1, keepdims=True)
    factor = lax.rsqrt(spread + EPSILON)
    return (centred * factor, factor)


def group_normalize(values):
    middle = jnp.mean(values, -1, keepdims=True)
    centred = values - middle
    spread = jnp.mean(centred * centred, -1, keepdims=True)
    factor = lax.rsqrt(jnp.maximum(spread, 1.0))
    active = jnp.where(spread > 1.0, 1.0, 0.0)
    return (centred * factor, factor, active)


def normalize_back(scaled, normed, factor, active=1.0):
    first_mean = jnp.mean(scaled, -1, keepdims=True)
    second_mean = jnp.mean(scaled * normed, -1, keepdims=True)
    return factor * (scaled - first_mean - active * normed * second_mean)


def silu_slope(values, sigma):
    return sigma * (1.0 + values * (1.0 - sigma))


def decay_rates(head_ids):
    return jnp.log(1.0 - jnp.exp2(-5.0 - head_ids.astype(F32)))


def decay_block(rate, size, blocks_apart):
    distance = (
        lax.broadcasted_iota(jnp.int32, (size, size), 0)
        - lax.broadcasted_iota(jnp.int32, (size, size), 1)
        + blocks_apart * size
    )
    decay = jnp.exp(jnp.maximum(distance, 0).astype(F32) * rate)
    return jnp.where(distance >= 0, decay, 0.0) if blocks_apart == 0 else decay


def project(first, first_full, third):
    length, width = first.shape
    total = first_full.shape[1]
    step = 512
    steps, low_steps = total // step, third // step

    def kernel(x_ref, w_ref, low_ref, high_ref):
        terms = dot(x_ref[...], w_ref[...], NN)

        @pl.when(pl.program_id(0) < low_steps)
        def _():
            low_ref[...] = terms.astype(BF16)

        @pl.when(pl.program_id(0) >= low_steps)
        def _():
            high_ref[...] = terms

    return pl.pallas_call(
        kernel,
        grid=(steps,),
        in_specs=[
            pl.BlockSpec((length, width), lambda n: (0, 0)),
            pl.BlockSpec((width, step), lambda n: (0, n)),
        ],
        out_specs=[
            pl.BlockSpec((length, step), lambda n: (0, jnp.minimum(n, low_steps - 1))),
            pl.BlockSpec((length, step), lambda n: (0, jnp.maximum(n - low_steps, 0))),
        ],
        out_shape=[
            jax.ShapeDtypeStruct((length, third), BF16),
            jax.ShapeDtypeStruct((length, total - third), F32),
        ],
        cost_estimate=COST,
        name="project",
    )(first, first_full)


def retain_mix(qkv, swish_pre, rates, ggain, gshift, query_width, value_width, places):
    length = qkv.shape[0]
    heads_here = rates.shape[0]
    narrow, wide = query_width // heads_here, value_width // heads_here
    block = 256
    count = length // block
    factor = narrow ** (-0.5)

    size = value_width // places.shape[0]
    chunks = wide // size

    def kernel(rate_ref, place_ref, q_ref, k_ref, v_ref, s_ref, gain_ref, shift_ref, r_ref, m_ref):
        rate = rate_ref[pl.program_id(0)]
        decays = [decay_block(rate, block, apart) for apart in range(count)]
        for i in range(count):
            rows = slice(i * block, (i + 1) * block)
            query = q_ref[rows, :]
            total = jnp.zeros((block, wide), F32)
            for j in range(i + 1):
                cols = slice(j * block, (j + 1) * block)
                weights = (dot(query, k_ref[cols, :], NT) * factor * decays[i - j]).astype(BF16)
                total += dot(weights, v_ref[cols, :], NN)
            retained = total.astype(BF16)
            r_ref[rows, :] = retained
            normed = group_normalize(retained.astype(F32))[0]
            swish = s_ref[rows, :]
            grouped = normed * gain_ref[...] + shift_ref[...]
            mixed = (grouped * (swish * jax.nn.sigmoid(swish))).astype(BF16)
            if size % 128:
                m_ref[rows, :] = mixed
            else:
                for k in range(chunks):
                    at = pl.multiple_of(place_ref[pl.program_id(0) * chunks + k] * size, size)
                    m_ref[rows, pl.ds(at, size)] = mixed[:, k * size : (k + 1) * size]

    def head(width, start):
        return pl.BlockSpec((length, width), lambda h: (0, start // width + h))

    flat = pl.BlockSpec((1, wide), lambda h: (0, h))
    moved = head(wide, 0) if size % 128 else pl.BlockSpec((length, value_width), lambda h: (0, 0))
    return pl.pallas_call(
        kernel,
        grid=(heads_here,),
        in_specs=[
            pl.BlockSpec(memory_space=pltpu.SMEM),
            pl.BlockSpec(memory_space=pltpu.SMEM),
            head(narrow, 0),
            head(narrow, query_width),
            head(wide, 2 * query_width),
            head(wide, 0),
            flat,
            flat,
        ],
        out_specs=[head(wide, 0), moved],
        out_shape=[jax.ShapeDtypeStruct((length, value_width), BF16)] * 2,
        cost_estimate=COST,
        name="retain_mix",
    )(rates, places, qkv, qkv, qkv, swish_pre, ggain[None], gshift[None])


def retain_back(qkv, dretained, rates, query_width, value_width, deps):
    length = qkv.shape[0]
    heads_here = rates.shape[0]
    narrow, wide = query_width // heads_here, value_width // heads_here
    block = 256
    count = length // block
    factor = narrow ** (-0.5)

    def kernel(rate_ref, q_ref, k_ref, v_ref, g_ref, *rest):
        dq_ref, dk_ref, dv_ref, acc_ref = rest[len(deps) :]
        rate = rate_ref[pl.program_id(0)]
        decays = [decay_block(rate, block, apart) for apart in range(count)]
        acc_ref[...] = jnp.zeros_like(acc_ref)
        for j in range(count):
            cols = slice(j * block, (j + 1) * block)
            key, value = k_ref[cols, :], v_ref[cols, :]
            dkey = jnp.zeros((block, narrow), F32)
            dvalue = jnp.zeros((block, wide), F32)
            for i in range(j, count):
                rows = slice(i * block, (i + 1) * block)
                query, grad = q_ref[rows, :], g_ref[rows, :]
                decay = decays[i - j]
                weights = (dot(query, key, NT) * factor * decay).astype(BF16)
                dvalue += dot(weights, grad, TN)
                dscores = (dot(grad, value, NT) * decay).astype(BF16)
                acc_ref[rows, :] += dot(dscores, key, NN)
                dkey += dot(dscores, query, TN)
            dk_ref[cols, :] = (dkey * factor).astype(BF16)
            dv_ref[cols, :] = dvalue.astype(BF16)
        dq_ref[...] = (acc_ref[...] * factor).astype(BF16)

    def head(width, start):
        return pl.BlockSpec((length, width), lambda h: (0, start // width + h))

    return pl.pallas_call(
        kernel,
        grid=(heads_here,),
        in_specs=[
            pl.BlockSpec(memory_space=pltpu.SMEM),
            head(narrow, 0),
            head(narrow, query_width),
            head(wide, 2 * query_width),
            head(wide, 0),
        ]
        + [UNREAD] * len(deps),
        out_specs=[head(narrow, 0), head(narrow, 0), head(wide, 0)],
        out_shape=[
            jax.ShapeDtypeStruct((length, query_width), BF16),
            jax.ShapeDtypeStruct((length, query_width), BF16),
            jax.ShapeDtypeStruct((length, value_width), BF16),
        ],
        scratch_shapes=[pltpu.VMEM((length, narrow), F32)],
        cost_estimate=COST,
        name="retain_back",
    )(rates, qkv, qkv, qkv, dretained, *deps)


def gate_back(grad, down_full, both, gbias, ubias, deps):
    length, width = grad.shape
    hidden = down_full.shape[0]
    block, rows = 256, 128
    steps = hidden // block

    def kernel(g_ref, w_ref, gate_ref, up_ref, gb_ref, ub_ref, *rest):
        dg_ref, du_ref, gsum_ref, usum_ref, acc_ref = rest[len(deps) :]
        acc_ref[...] = dot(g_ref[...], w_ref[...], NT)
        gsum_ref[...] = jnp.zeros_like(gsum_ref)
        usum_ref[...] = jnp.zeros_like(usum_ref)

        @pl.loop(0, length // rows)
        def _(i):
            at = pl.ds(pl.multiple_of(i * rows, rows), rows)
            dhidden = acc_ref[at, :]
            gating, upward = gate_ref[at, :] + gb_ref[...], up_ref[at, :] + ub_ref[...]
            sigma = jax.nn.sigmoid(gating)
            dgating = (dhidden * upward * silu_slope(gating, sigma)).astype(BF16)
            dupward = (dhidden * (gating * sigma)).astype(BF16)
            dg_ref[at, :] = dgating
            du_ref[at, :] = dupward
            gsum_ref[...] += jnp.sum(dgating.astype(F32), 0, keepdims=True)
            usum_ref[...] += jnp.sum(dupward.astype(F32), 0, keepdims=True)

    tall = pl.BlockSpec((length, block), lambda j: (0, j))
    flat = pl.BlockSpec((1, block), lambda j: (0, j))
    return pl.pallas_call(
        kernel,
        grid=(steps,),
        in_specs=[
            pl.BlockSpec((length, width), lambda j: (0, 0)),
            pl.BlockSpec((block, width), lambda j: (j, 0)),
            tall,
            pl.BlockSpec((length, block), lambda j: (0, steps + j)),
            flat,
            flat,
        ]
        + [UNREAD] * len(deps),
        out_specs=[tall, tall, flat, flat],
        out_shape=[jax.ShapeDtypeStruct((length, hidden), BF16)] * 2
        + [jax.ShapeDtypeStruct((1, hidden), F32)] * 2,
        scratch_shapes=[pltpu.VMEM((length, block), F32)],
        cost_estimate=COST,
        name="gate_back",
    )(grad, down_full, both, both, gbias[None], ubias[None], *deps)


def mixed_back(dres_low, out_full, retained, swish_pre, ggain, gshift, heads_here, places, deps):
    length, width = dres_low.shape
    value_width = out_full.shape[0]
    block, rows = value_width // heads_here, 128

    size = value_width // places.shape[0]
    chunks = block // size
    aligned = size % 128 == 0

    def kernel(place_ref, d_ref, w_ref, r_ref, s_ref, gain_ref, shift_ref, *rest):
        ds_ref, dr_ref, gsum_ref, ssum_ref, acc_ref, head_ref = rest[len(deps) :]
        if aligned:
            for k in range(chunks):
                at = pl.multiple_of(place_ref[pl.program_id(0) * chunks + k] * size, size)
                head_ref[k * size : (k + 1) * size, :] = w_ref[pl.ds(at, size), :]
            acc_ref[...] = dot(d_ref[...], head_ref[...], NT)
        else:
            acc_ref[...] = dot(d_ref[...], w_ref[...], NT)
        gsum_ref[...] = jnp.zeros_like(gsum_ref)
        ssum_ref[...] = jnp.zeros_like(ssum_ref)

        @pl.loop(0, length // rows)
        def _(i):
            at = pl.ds(pl.multiple_of(i * rows, rows), rows)
            dmixed = acc_ref[at, :]
            normed, factor, active = group_normalize(r_ref[at, :].astype(F32))
            swish = s_ref[at, :]
            sigma = jax.nn.sigmoid(swish)
            dgrouped = dmixed * (swish * sigma)
            grouped = normed * gain_ref[...] + shift_ref[...]
            ds_ref[at, :] = (dmixed * grouped * silu_slope(swish, sigma)).astype(BF16)
            gsum_ref[...] += jnp.sum(dgrouped * normed, 0, keepdims=True)
            ssum_ref[...] += jnp.sum(dgrouped, 0, keepdims=True)
            dr_ref[at, :] = normalize_back(dgrouped * gain_ref[...], normed, factor, active).astype(BF16)

    tall = pl.BlockSpec((length, block), lambda h: (0, h))
    flat = pl.BlockSpec((1, block), lambda h: (0, h))
    return pl.pallas_call(
        kernel,
        grid=(heads_here,),
        in_specs=[
            pl.BlockSpec(memory_space=pltpu.SMEM),
            pl.BlockSpec((length, width), lambda h: (0, 0)),
            pl.BlockSpec((value_width, width), lambda h: (0, 0))
            if aligned
            else pl.BlockSpec((block, width), lambda h: (h, 0)),
            tall,
            tall,
            flat,
            flat,
        ]
        + [UNREAD] * len(deps),
        out_specs=[tall, tall, flat, flat],
        out_shape=[jax.ShapeDtypeStruct((length, value_width), BF16)] * 2
        + [jax.ShapeDtypeStruct((1, value_width), F32)] * 2,
        scratch_shapes=[pltpu.VMEM((length, block), F32), pltpu.VMEM((block, width), BF16)],
        cost_estimate=COST,
        name="mixed_back",
    )(places, dres_low, out_full, retained, swish_pre, ggain[None], gshift[None], *deps)


def full_product(lefts, rights, dims, wide, deps):
    length = lefts[0].shape[0]
    step = min(wide, 512)
    specs = [pl.BlockSpec((length, left.shape[1]), lambda n: (0, 0)) for left in lefts]
    for left, (_, column) in zip(lefts, rights):
        depth = left.shape[1]
        if dims is NT:
            specs.append(pl.BlockSpec((step, depth), lambda n, c=column: (n, c)))
        else:
            specs.append(pl.BlockSpec((depth, step), lambda n: (0, n)))

    def kernel(*refs):
        total = dot(refs[0][...], refs[len(lefts)][...], dims)
        for k in range(1, len(lefts)):
            total += dot(refs[k][...], refs[len(lefts) + k][...], dims)
        refs[-1][...] = total.astype(BF16)

    return pl.pallas_call(
        kernel,
        grid=(wide // step,),
        in_specs=specs + [UNREAD] * len(deps),
        out_specs=pl.BlockSpec((length, step), lambda n: (0, n)),
        out_shape=jax.ShapeDtypeStruct((length, wide), BF16),
        cost_estimate=COST,
        name="full_product",
    )(*lefts, *[right for right, _ in rights], *deps)


class Ring:
    def __init__(self, size):
        half = size // 2
        self.size = size
        self.half = half
        self.order = list(range(half)) + list(range(size - 1, half - 1, -1))
        place = [0] * size
        for position, rank in enumerate(self.order):
            place[rank] = position
        self.right = [(self.order[i], self.order[(i + 1) % size]) for i in range(size)]
        self.left = [(self.order[i], self.order[(i - 1) % size]) for i in range(size)]
        self.me = lax.axis_index("sp")
        self.position = jnp.array(place, jnp.int32)[self.me]

    def rank(self, step):
        return jnp.array(self.order, jnp.int32)[lax.rem(self.position + step + self.size, self.size)]

    def ranks(self, *steps):
        return jnp.stack([self.rank(step) for step in steps])

    def to_right(self, block):
        return lax.ppermute(block, "sp", self.right)

    def to_left(self, block):
        return lax.ppermute(block, "sp", self.left)

    def pieces(self, block):
        middle = block.shape[0] // 2
        found = [(0, block)]
        from_left, from_right = block, block
        for step in range(1, self.half):
            from_left, from_right = self.to_right(from_left), self.to_left(from_right)
            found += [(-step, from_left), (step, from_right)]
        low = self.to_right(from_left[:middle])
        high = self.to_left(from_right[middle:])
        return found, low, high

    def gather(self, block, base=None):
        found, low, high = self.pieces(block)
        if base is None:
            out = jnp.zeros((self.size,) + block.shape, block.dtype)
        else:
            out = after(base, *[part for _, part in found]).reshape((self.size,) + block.shape)
        found.append((self.half, jnp.concatenate([low, high], 0)))
        for step, part in found:
            out = lax.dynamic_update_slice(out, part[None], (self.rank(step), 0, 0))
        return out.reshape(self.size * block.shape[0], block.shape[1])

    def gather_columns(self, pieces, outs, deps):
        found, low, high = pieces
        block = found[0][1]
        rows = block.shape[0]
        widths = [width for width, _ in outs]
        if any(chunk % 128 for _, chunk in outs):
            found.append((self.half, jnp.concatenate([low, high], 0)))
            whole = jnp.zeros((self.size,) + block.shape, block.dtype)
            for step, part in found:
                whole = lax.dynamic_update_slice(whole, part[None], (self.rank(step), 0, 0))
            results, start = [], 0
            for width, chunk in outs:
                share = whole[:, :, start : start + width].reshape(self.size, rows, -1, chunk)
                share = share.transpose(1, 2, 0, 3).reshape(rows, -1)
                results.append(share.astype(F32))
                start += width
            return results
        step_rows = min(64, rows // 2)
        steps = rows // step_rows
        middle = steps // 2
        size = self.size
        ranks = self.ranks(*[step for step, _ in found], self.half)

        def kernel(rank_ref, *refs):
            sources, out_refs = refs[: len(found) + 2], refs[len(found) + 2 + len(deps) :]

            def put(source, rank):
                start = 0
                for (width, chunk), out_ref in zip(outs, out_refs):
                    for k in range(width // chunk):
                        at = pl.multiple_of(k * size * chunk + rank * chunk, 128)
                        piece = source[:, start + k * chunk : start + (k + 1) * chunk]
                        out_ref[:, pl.ds(at, chunk)] = piece.astype(F32)
                    start += width

            for k in range(len(found)):
                put(sources[k], rank_ref[k])

            @pl.when(pl.program_id(0) < middle)
            def _():
                put(sources[-2], rank_ref[len(found)])

            @pl.when(pl.program_id(0) >= middle)
            def _():
                put(sources[-1], rank_ref[len(found)])

        total = block.shape[1]
        in_specs = [pl.BlockSpec((step_rows, total), lambda i, r: (i, 0)) for _ in found]
        in_specs.append(pl.BlockSpec((step_rows, total), lambda i, r: (jnp.minimum(i, middle - 1), 0)))
        in_specs.append(pl.BlockSpec((step_rows, total), lambda i, r: (jnp.maximum(i - middle, 0), 0)))
        return pl.pallas_call(
            kernel,
            grid_spec=pltpu.PrefetchScalarGridSpec(
                num_scalar_prefetch=1,
                grid=(steps,),
                in_specs=in_specs + [UNREAD] * len(deps),
                out_specs=[pl.BlockSpec((step_rows, size * width), lambda i, r: (i, 0)) for width in widths],
            ),
            out_shape=[jax.ShapeDtypeStruct((rows, size * width), F32) for width in widths],
            cost_estimate=COST,
            name="gather_columns",
        )(ranks, *[part for _, part in found], low, high, *deps)

    def gather_rows(self, pieces, deps):
        found, low, high = pieces
        rows, wide = found[0][1].shape
        step = min(wide, 512)
        parts = [part for _, part in found] + [low, high]
        ranks = self.ranks(*[place for place, _ in found], self.half)

        def kernel(rank_ref, *refs):
            out_ref = refs[-1]
            for k in range(len(found) + 2):
                size = parts[k].shape[0]
                at = rank_ref[min(k, len(found))] * rows
                if k == len(found) + 1:
                    at = at + rows - size
                out_ref[pl.ds(pl.multiple_of(at, size), size), :] = refs[k][...].astype(F32)

        return pl.pallas_call(
            kernel,
            grid_spec=pltpu.PrefetchScalarGridSpec(
                num_scalar_prefetch=1,
                grid=(wide // step,),
                in_specs=[pl.BlockSpec((part.shape[0], step), lambda n, r: (0, n)) for part in parts]
                + [UNREAD] * len(deps),
                out_specs=pl.BlockSpec((self.size * rows, step), lambda n, r: (0, n)),
            ),
            out_shape=jax.ShapeDtypeStruct((self.size * rows, wide), F32),
            cost_estimate=COST,
            name="gather_rows",
        )(ranks, *parts, *deps)

    def rows_of(self, terms, step):
        rows = terms.shape[0] // self.size
        return lax.dynamic_slice_in_dim(terms, self.rank(step) * rows, rows, 0)

    def sum_far(self, terms, *others):
        far = self.rows_of(terms, self.half)
        middle = far.shape[0] // 2
        low, high = far[:middle], far[middle:]
        if others:
            low, high = after(low, *others), after(high, *others)
        return (low, high), (self.to_right(low), self.to_left(high))

    def sum_near(self, terms, arrived, *others):
        from_left, from_right = arrived
        for step in range(self.half - 1, 0, -1):
            ahead = self.rows_of(terms, step).astype(F32)
            behind = self.rows_of(terms, -step).astype(F32)
            rows, part = ahead.shape[0], from_left.shape[0]
            ahead = ahead + jnp.pad(from_left.astype(F32), ((0, rows - part), (0, 0)))
            behind = behind + jnp.pad(from_right.astype(F32), ((rows - part, 0), (0, 0)))
            ahead, behind = ahead.astype(BF16), behind.astype(BF16)
            from_left, from_right = self.to_right(ahead), self.to_left(behind)
        return (ahead, behind), (from_left, from_right)

    def sum_own(self, terms, arrived):
        return self.rows_of(terms, 0).astype(F32) + arrived[0].astype(F32) + arrived[1].astype(F32)

    def scatter_sum(self, terms):
        return self.sum_own(terms, self.sum_near(terms, self.sum_far(terms)[1])[1])


class Line:
    def __init__(self, shards):
        self.shards = shards
        self.chips = shards // 2
        index = lax.axis_index("fsdp")
        self.core = lax.rem(index, 2)
        self.groups = [[2 * i + core for i in range(self.chips)] for core in range(2)]
        self.swap = [(i, i ^ 1) for i in range(shards)]

    def to_core(self, block):
        return lax.ppermute(block, "fsdp", self.swap)

    def half(self, left, rights, core, other, deps):
        length = left.shape[0]
        rows = left.shape[1] // self.shards
        wide = sum(right.shape[1] for right in rights)
        if rows % 128:
            columns = [
                lax.dynamic_slice_in_dim(left, (2 * i + core) * rows, rows, 1) for i in range(self.chips)
            ]
            left = after(jnp.concatenate(columns, 1), *deps)
            total = over_rows(left, jnp.concatenate(rights, 1))
            if other is not None:
                total = total + other.astype(F32)
            return total.astype(BF16)
        extra = [] if other is None else [other]

        def kernel(core_ref, x_ref, *refs):
            out_ref = refs[-1]
            start = 0
            for ref, right in zip(refs, rights):
                size = right.shape[1]
                total = dot(x_ref[...], ref[...], TN)
                if extra:
                    total += refs[len(rights)][:, start : start + size].astype(F32)
                out_ref[:, start : start + size] = total.astype(BF16)
                start += size

        return pl.pallas_call(
            kernel,
            grid_spec=pltpu.PrefetchScalarGridSpec(
                num_scalar_prefetch=1,
                grid=(self.chips,),
                in_specs=[pl.BlockSpec((length, rows), lambda i, c: (0, 2 * i + c[0]))]
                + [pl.BlockSpec((length, right.shape[1]), lambda i, c: (0, 0)) for right in rights]
                + [pl.BlockSpec((rows, wide), lambda i, c: (i, 0)) for _ in extra]
                + [UNREAD] * len(deps),
                out_specs=pl.BlockSpec((rows, wide), lambda i, c: (i, 0)),
            ),
            out_shape=jax.ShapeDtypeStruct((self.chips * rows, wide), BF16),
            cost_estimate=COST,
            name="rows_sum",
        )(core.reshape(1), left, *rights, *extra, *deps)

    def theirs(self, left, rights, deps):
        return self.half(left, rights, 1 - self.core, None, deps)

    def mine(self, left, rights, sent, deps):
        return self.half(left, rights, self.core, self.to_core(sent), deps)

    def scatter(self, block):
        return lax.psum_scatter(
            block, "fsdp", scatter_dimension=0, tiled=True, axis_index_groups=self.groups
        )


def butterfly(vector, axes=("fsdp", "sp")):
    for axis in axes:
        size = lax.axis_size(axis)
        step = 1
        while step < size:
            vector = vector + lax.ppermute(vector, axis, [(i, i ^ step) for i in range(size)])
            step *= 2
    return vector


class Spread:
    def __init__(self, shards, parts):
        chips = shards // 2
        assert chips == parts
        if parts == 4:
            moves = [[0, 2, 1, 3], [1, 3, 0, 2], [2, 0, 3, 1], [3, 1, 2, 0]]
        else:
            moves = [[(chip + rank) % chips for chip in range(chips)] for rank in range(parts)]
        self.along, self.across = [], []
        self.places = [[0] * shards for _ in range(parts)]
        self.pieces = [[0] * shards for _ in range(parts)]
        for rank, move in enumerate(moves):
            for chip, target in enumerate(move):
                for core in range(2):
                    middle = (2 * target + core) * parts + rank
                    self.along.append(((2 * chip + core) * parts + rank, middle))
                    self.across.append((middle, (2 * target + core) * parts + chip))
                    piece = core * parts + rank
                    self.places[chip][piece] = 2 * target + core
                    self.pieces[chip][2 * target + core] = piece

    def forth(self, block):
        block = lax.ppermute(block, ("fsdp", "sp"), self.along)
        return lax.ppermute(block, ("fsdp", "sp"), self.across)

    def back(self, block):
        block = lax.ppermute(block, ("fsdp", "sp"), [(there, here) for here, there in self.across])
        return lax.ppermute(block, ("fsdp", "sp"), [(there, here) for here, there in self.along])


def reorder(array, order, size, axis):
    chunks = [
        lax.dynamic_slice_in_dim(array, order[i] * size, size, axis)
        for i in range(array.shape[axis] // size)
    ]
    return jnp.concatenate(chunks, axis)


def local(
    tokens,
    attn_gain,
    attn_shift,
    query_weight,
    key_weight,
    value_weight,
    swish_weight,
    group_gain,
    group_shift,
    out_weight,
    ffn_gain,
    ffn_shift,
    gating_weight,
    upward_weight,
    gating_bias,
    upward_bias,
    downward_weight,
    downward_bias,
    cotangent,
):
    seq_count, local_len, width = tokens.shape
    assert seq_count == 1
    parts = lax.axis_size("sp")
    shards = lax.axis_size("fsdp")
    me = lax.axis_index("sp")
    ring = Ring(parts)
    line = Line(shards)
    heads_here = HEADS // parts
    full_len = local_len * parts
    value_all = value_weight.shape[1]
    hidden_all = gating_weight.shape[1]
    value_width = value_all // parts
    hidden_width = hidden_all // parts
    query_width = query_weight.shape[1] // parts
    third = 2 * query_width + value_width
    chunk = hidden_width // shards

    def columns(weight):
        size = weight.shape[1] // parts
        return lax.dynamic_slice_in_dim(weight, me * size, size, 1)

    def units(weight):
        pieces = [
            lax.dynamic_slice_in_dim(weight, (i * parts + me) * chunk, chunk, weight.ndim - 1)
            for i in range(shards)
        ]
        return jnp.concatenate(pieces, -1)

    def gathered(array):
        return lax.all_gather(array, "fsdp", axis=0, tiled=True)

    small = [
        attn_gain, attn_shift, group_gain, group_shift, ffn_gain, ffn_shift,
        gating_bias, upward_bias, downward_bias,
    ]
    sizes = [item.shape[0] for item in small]
    stacked = jnp.zeros((shards, sum(sizes)), BF16)
    stacked = lax.dynamic_update_slice(
        stacked, jnp.concatenate(small, 0)[None], (lax.axis_index("fsdp"), 0)
    )
    stacked = butterfly(stacked, ("fsdp",))
    offsets = [sum(sizes[:i]) for i in range(len(sizes))]
    (
        gain_one, shift_one, ggain_all, gshift_all, gain_two, shift_two, gbias_all, ubias_all, dbias,
    ) = (
        stacked[:, start : start + size].reshape(-1).astype(F32)
        for start, size in zip(offsets, sizes)
    )
    ggain = lax.dynamic_slice_in_dim(ggain_all, me * value_width, value_width, 0)
    gshift = lax.dynamic_slice_in_dim(gshift_all, me * value_width, value_width, 0)
    gbias = units(gbias_all)
    ubias = units(ubias_all)

    tokens_all = ring.gather(tokens.reshape(-1, width))
    flat = tokens.reshape(-1, width).astype(F32)
    first_norm, first_factor = normalize(flat)
    first = normalize(tokens_all.astype(F32))[0]
    first = (first * gain_one + shift_one).astype(BF16)
    grad_own = cotangent.reshape(-1, width)
    grad_low = ring.gather(after(grad_own, first))

    first_full = gathered(
        jnp.concatenate(
            [columns(query_weight), columns(key_weight), columns(value_weight), columns(swish_weight)], 1
        )
    )
    spread = Spread(shards, parts)
    places = jnp.array(spread.places, jnp.int32)[me]
    rows = out_weight.shape[0] // parts
    out_piece = spread.forth(lax.dynamic_slice_in_dim(out_weight, me * rows, rows, 0))
    out_full = gathered(after(out_piece, first))
    both_full = gathered(jnp.concatenate([units(gating_weight), units(upward_weight)], 1))
    down_full = gathered(lax.dynamic_slice_in_dim(downward_weight, me * rows, rows, 0))

    qkv, swish_pre = project(first, first_full, third)
    rates = decay_rates(me * heads_here + jnp.arange(heads_here))
    retained, mixed = retain_mix(qkv, swish_pre, rates, ggain, gshift, query_width, value_width, places)
    out_ordered = out_full
    if rows % 128:
        mixed = reorder(mixed, jnp.array(spread.pieces, jnp.int32)[me], rows, 1)
        out_ordered = reorder(out_full, places, rows, 0)
    mixed = after(mixed, grad_low)

    terms = full_product([mixed], [(out_full, 0)], NN, width, ())
    resid = flat + ring.scatter_sum(terms)
    spare = terms
    second_norm, second_factor = normalize(resid)
    second = ring.gather((second_norm * gain_two + shift_two).astype(BF16), tokens_all)
    both = product(second, both_full)
    hidden = (jax.nn.silu(both[:, :hidden_width] + gbias) * (both[:, hidden_width:] + ubias)).astype(BF16)

    sent = line.theirs(hidden, [grad_low], ())
    down_sum = line.mine(hidden, [grad_low], sent, ())
    down_share = line.scatter(down_sum)
    dgating, dupward, gbias_term, ubias_term = gate_back(
        grad_low, down_full, both, gbias, ubias, (down_sum,)
    )
    terms = full_product([dgating, dupward], [(both_full, 0), (both_full, 1)], NT, width, ())
    far, arrived = ring.sum_far(terms)
    sent = line.theirs(second, [dgating, dupward], far)
    arrived = lax.optimization_barrier(arrived + (down_share,))[:2]
    near, arrived = ring.sum_near(terms, arrived)
    both_sum = line.mine(second, [dgating, dupward], sent, near)
    both_share = line.scatter(both_sum)
    result = full_product([hidden], [(down_full, 0)], NN, width, (both_sum,))
    dsecond = ring.sum_own(after(terms, result), arrived)
    fgain_term = jnp.sum(dsecond * second_norm, 0)
    fshift_term = jnp.sum(dsecond, 0)
    grad_out = grad_own.astype(F32)
    dbias_term = jnp.sum(grad_out, 0)
    dresid = grad_out + normalize_back(dsecond * gain_two, second_norm, second_factor)

    dres_own = dresid.astype(BF16)
    dres_low = ring.gather(dres_own, spare)
    sent = line.theirs(mixed, [dres_low], ())
    far, result_far = ring.sum_far(result, dres_low)
    out_sum = line.mine(mixed, [dres_low], sent, far)
    out_share = line.scatter(out_sum)
    both_pieces = ring.pieces(after(both_share, out_sum))
    both_near = tuple(part for _, part in both_pieces[0])
    dswish, dretained, ggain_term, gshift_term = mixed_back(
        dres_low, out_ordered, retained, swish_pre, ggain, gshift, heads_here, places, (out_sum, both_share)
    )
    dquery, dkey, dvalue = retain_back(qkv, dretained, rates, query_width, value_width, ())
    result_far = lax.optimization_barrier(result_far + (dvalue,))[:2]
    near, result_near = ring.sum_near(result, result_far)
    sent = line.theirs(first, [dvalue, dswish], near + both_near)
    sent_qk = line.theirs(first, [dquery, dkey], (sent, out_share))
    out_share = spread.back(out_share)
    vs_sum = line.mine(first, [dvalue, dswish], sent, (sent_qk, out_share))
    vs_share = line.scatter(vs_sum)
    rights = [(first_full, 0), (first_full, 1), (first_full, 2 * query_width // value_width)]
    rights.append((first_full, third // value_width))
    terms = full_product([dquery, dkey, dvalue, dswish], rights, NT, width, (vs_sum,))
    far, arrived = ring.sum_far(terms)
    down_pieces = ring.pieces(after(down_share, sent))
    qk_sum = line.mine(first, [dquery, dkey], sent_qk, far)
    qk_share = line.scatter(qk_sum)
    result = ring.sum_own(after(result, qk_sum), result_near)
    layer_out = (resid + result + dbias).astype(BF16)
    arrived = lax.optimization_barrier(arrived + (layer_out,))[:2]
    near, arrived = ring.sum_near(terms, arrived)
    gating_grad, upward_grad = ring.gather_columns(
        both_pieces, [(hidden_width, chunk), (hidden_width, chunk)], near
    )
    dfirst = ring.sum_own(after(terms, gating_grad), arrived)
    again_term = jnp.sum(dfirst * first_norm, 0)
    ashift_term = jnp.sum(dfirst, 0)
    input_grad = dresid + normalize_back(dfirst * gain_one, first_norm, first_factor)

    downward_grad = ring.gather_rows(down_pieces, (dfirst,))
    out_grad = ring.gather_rows(ring.pieces(after(out_share, *near)), (downward_grad,))
    vs_pieces = ring.pieces(vs_share)
    value_grad, swish_grad = ring.gather_columns(
        vs_pieces, [(value_width, value_width), (value_width, value_width)], ()
    )
    query_grad, key_grad = ring.gather_columns(
        ring.pieces(qk_share), [(query_width, query_width), (query_width, query_width)], (value_grad,)
    )

    def placed(term, whole):
        return lax.dynamic_update_slice(jnp.zeros((whole,), F32), term, (me * term.shape[0],))

    def placed_units(term):
        blank = jnp.zeros((shards, parts, chunk), F32)
        return lax.dynamic_update_slice(blank, term.reshape(shards, 1, chunk), (0, me, 0)).reshape(-1)

    terms = [
        again_term, ashift_term, placed(ggain_term[0], value_all), placed(gshift_term[0], value_all),
        fgain_term, fshift_term, placed_units(gbias_term[0]), placed_units(ubias_term[0]), dbias_term,
    ]
    terms = jnp.concatenate([term.reshape(shards, -1) for term in terms], 1)
    totals = butterfly(after(butterfly(after(terms, *[part for _, part in vs_pieces[0]]), ("fsdp",)), qk_share), ("sp",))
    mine = lax.dynamic_slice_in_dim(totals, lax.axis_index("fsdp"), 1, 0)[0]
    (
        again_grad, ashift_grad, ggain_grad, gshift_grad, fgain_grad, fshift_grad,
        gbias_grad, ubias_grad, dbias_grad,
    ) = (mine[start : start + size] for start, size in zip(offsets, sizes))
    return (
        layer_out.reshape(seq_count, local_len, width),
        input_grad.reshape(seq_count, local_len, width),
        again_grad,
        ashift_grad,
        query_grad,
        key_grad,
        value_grad,
        swish_grad,
        ggain_grad,
        gshift_grad,
        out_grad,
        fgain_grad,
        fshift_grad,
        gating_grad,
        upward_grad,
        gbias_grad,
        ubias_grad,
        downward_grad,
        dbias_grad,
    )


def solution(mesh):
    row, vector, cube = P("fsdp", None), P("fsdp"), P("fsdp", "sp", None)
    return jax.shard_map(
        local,
        mesh=mesh,
        in_specs=(
            cube, vector, vector, row, row, row, row, vector, vector, row,
            vector, vector, row, row, vector, vector, row, vector, cube,
        ),
        out_specs=(
            cube, cube, vector, vector, row, row, row, row, vector, vector,
            row, vector, vector, row, row, vector, vector, row, vector,
        ),
        check_vma=False,
    )
```

```python
import functools

import jax
import jax.numpy as jnp
from jax import lax
from jax.experimental import pallas as pl
from jax.experimental.pallas import tpu as pltpu
from jax.sharding import PartitionSpec as P

HEADS = 8
EPSILON = 1e-05
BF16 = jnp.bfloat16
F32 = jnp.float32
COST = pl.CostEstimate(flops=1024, bytes_accessed=1024, transcendentals=0)
UNREAD = pl.BlockSpec(memory_space=pl.ANY)
NT = (((1,), (1,)), ((), ()))
NN = (((1,), (0,)), ((), ()))
TN = (((0,), (0,)), ((), ()))


def dot(left, right, dims):
    return lax.dot_general(left, right, dims, preferred_element_type=F32)


def product(left, right):
    return dot(left, right, NN)


def over_rows(left, right):
    return dot(left, right, TN)


def after(value, *others):
    return lax.optimization_barrier((value,) + others)[0]


def normalize(values):
    middle = jnp.mean(values, -1, keepdims=True)
    centred = values - middle
    spread = jnp.mean(centred * centred, -1, keepdims=True)
    factor = lax.rsqrt(spread + EPSILON)
    return (centred * factor, factor)


def group_normalize(values):
    middle = jnp.mean(values, -1, keepdims=True)
    centred = values - middle
    spread = jnp.mean(centred * centred, -1, keepdims=True)
    factor = lax.rsqrt(jnp.maximum(spread, 1.0))
    active = jnp.where(spread > 1.0, 1.0, 0.0)
    return (centred * factor, factor, active)


def normalize_back(scaled, normed, factor, active=1.0):
    first_mean = jnp.mean(scaled, -1, keepdims=True)
    second_mean = jnp.mean(scaled * normed, -1, keepdims=True)
    return factor * (scaled - first_mean - active * normed * second_mean)


def silu_slope(values, sigma):
    return sigma * (1.0 + values * (1.0 - sigma))


def decay_rates(head_ids):
    return jnp.log(1.0 - jnp.exp2(-5.0 - head_ids.astype(F32)))


def decay_block(rate, size, blocks_apart):
    distance = (
        lax.broadcasted_iota(jnp.int32, (size, size), 0)
        - lax.broadcasted_iota(jnp.int32, (size, size), 1)
        + blocks_apart * size
    )
    decay = jnp.exp(jnp.maximum(distance, 0).astype(F32) * rate)
    return jnp.where(distance >= 0, decay, 0.0) if blocks_apart == 0 else decay


def project(first, first_full, third):
    length, width = first.shape
    total = first_full.shape[1]
    step = 512
    steps, low_steps = total // step, third // step

    def kernel(x_ref, w_ref, low_ref, high_ref):
        terms = dot(x_ref[...], w_ref[...], NN)

        @pl.when(pl.program_id(0) < low_steps)
        def _():
            low_ref[...] = terms.astype(BF16)

        @pl.when(pl.program_id(0) >= low_steps)
        def _():
            high_ref[...] = terms

    return pl.pallas_call(
        kernel,
        grid=(steps,),
        in_specs=[
            pl.BlockSpec((length, width), lambda n: (0, 0)),
            pl.BlockSpec((width, step), lambda n: (0, n)),
        ],
        out_specs=[
            pl.BlockSpec((length, step), lambda n: (0, jnp.minimum(n, low_steps - 1))),
            pl.BlockSpec((length, step), lambda n: (0, jnp.maximum(n - low_steps, 0))),
        ],
        out_shape=[
            jax.ShapeDtypeStruct((length, third), BF16),
            jax.ShapeDtypeStruct((length, total - third), F32),
        ],
        cost_estimate=COST,
        name="project",
    )(first, first_full)


def retain_mix(qkv, swish_pre, rates, ggain, gshift, query_width, value_width, places):
    length = qkv.shape[0]
    heads_here = rates.shape[0]
    narrow, wide = query_width // heads_here, value_width // heads_here
    block = 256
    count = length // block
    factor = narrow ** (-0.5)

    size = value_width // places.shape[0]
    chunks = wide // size

    def kernel(rate_ref, place_ref, q_ref, k_ref, v_ref, s_ref, gain_ref, shift_ref, r_ref, m_ref):
        rate = rate_ref[pl.program_id(0)]
        decays = [decay_block(rate, block, apart) for apart in range(count)]
        for i in range(count):
            rows = slice(i * block, (i + 1) * block)
            query = q_ref[rows, :]
            total = jnp.zeros((block, wide), F32)
            for j in range(i + 1):
                cols = slice(j * block, (j + 1) * block)
                weights = (dot(query, k_ref[cols, :], NT) * factor * decays[i - j]).astype(BF16)
                total += dot(weights, v_ref[cols, :], NN)
            retained = total.astype(BF16)
            r_ref[rows, :] = retained
            normed = group_normalize(retained.astype(F32))[0]
            swish = s_ref[rows, :]
            grouped = normed * gain_ref[...] + shift_ref[...]
            mixed = (grouped * (swish * jax.nn.sigmoid(swish))).astype(BF16)
            if size % 128:
                m_ref[rows, :] = mixed
            else:
                for k in range(chunks):
                    at = pl.multiple_of(place_ref[pl.program_id(0) * chunks + k] * size, size)
                    m_ref[rows, pl.ds(at, size)] = mixed[:, k * size : (k + 1) * size]

    def head(width, start):
        return pl.BlockSpec((length, width), lambda h: (0, start // width + h))

    flat = pl.BlockSpec((1, wide), lambda h: (0, h))
    moved = head(wide, 0) if size % 128 else pl.BlockSpec((length, value_width), lambda h: (0, 0))
    return pl.pallas_call(
        kernel,
        grid=(heads_here,),
        in_specs=[
            pl.BlockSpec(memory_space=pltpu.SMEM),
            pl.BlockSpec(memory_space=pltpu.SMEM),
            head(narrow, 0),
            head(narrow, query_width),
            head(wide, 2 * query_width),
            head(wide, 0),
            flat,
            flat,
        ],
        out_specs=[head(wide, 0), moved],
        out_shape=[jax.ShapeDtypeStruct((length, value_width), BF16)] * 2,
        cost_estimate=COST,
        name="retain_mix",
    )(rates, places, qkv, qkv, qkv, swish_pre, ggain[None], gshift[None])


def retain_back(qkv, dretained, rates, query_width, value_width, deps):
    length = qkv.shape[0]
    heads_here = rates.shape[0]
    narrow, wide = query_width // heads_here, value_width // heads_here
    block = 256
    count = length // block
    factor = narrow ** (-0.5)

    def kernel(rate_ref, q_ref, k_ref, v_ref, g_ref, *rest):
        dq_ref, dk_ref, dv_ref, acc_ref = rest[len(deps) :]
        rate = rate_ref[pl.program_id(0)]
        decays = [decay_block(rate, block, apart) for apart in range(count)]
        acc_ref[...] = jnp.zeros_like(acc_ref)
        for j in range(count):
            cols = slice(j * block, (j + 1) * block)
            key, value = k_ref[cols, :], v_ref[cols, :]
            dkey = jnp.zeros((block, narrow), F32)
            dvalue = jnp.zeros((block, wide), F32)
            for i in range(j, count):
                rows = slice(i * block, (i + 1) * block)
                query, grad = q_ref[rows, :], g_ref[rows, :]
                decay = decays[i - j]
                weights = (dot(query, key, NT) * factor * decay).astype(BF16)
                dvalue += dot(weights, grad, TN)
                dscores = (dot(grad, value, NT) * decay).astype(BF16)
                acc_ref[rows, :] += dot(dscores, key, NN)
                dkey += dot(dscores, query, TN)
            dk_ref[cols, :] = (dkey * factor).astype(BF16)
            dv_ref[cols, :] = dvalue.astype(BF16)
        dq_ref[...] = (acc_ref[...] * factor).astype(BF16)

    def head(width, start):
        return pl.BlockSpec((length, width), lambda h: (0, start // width + h))

    return pl.pallas_call(
        kernel,
        grid=(heads_here,),
        in_specs=[
            pl.BlockSpec(memory_space=pltpu.SMEM),
            head(narrow, 0),
            head(narrow, query_width),
            head(wide, 2 * query_width),
            head(wide, 0),
        ]
        + [UNREAD] * len(deps),
        out_specs=[head(narrow, 0), head(narrow, 0), head(wide, 0)],
        out_shape=[
            jax.ShapeDtypeStruct((length, query_width), BF16),
            jax.ShapeDtypeStruct((length, query_width), BF16),
            jax.ShapeDtypeStruct((length, value_width), BF16),
        ],
        scratch_shapes=[pltpu.VMEM((length, narrow), F32)],
        cost_estimate=COST,
        name="retain_back",
    )(rates, qkv, qkv, qkv, dretained, *deps)


def gate_back(grad, down_full, both, gbias, ubias, deps):
    length, width = grad.shape
    hidden = down_full.shape[0]
    block, rows = 256, 128
    steps = hidden // block

    def kernel(g_ref, w_ref, gate_ref, up_ref, gb_ref, ub_ref, *rest):
        dg_ref, du_ref, gsum_ref, usum_ref, acc_ref = rest[len(deps) :]
        acc_ref[...] = dot(g_ref[...], w_ref[...], NT)
        gsum_ref[...] = jnp.zeros_like(gsum_ref)
        usum_ref[...] = jnp.zeros_like(usum_ref)

        @pl.loop(0, length // rows)
        def _(i):
            at = pl.ds(pl.multiple_of(i * rows, rows), rows)
            dhidden = acc_ref[at, :]
            gating, upward = gate_ref[at, :] + gb_ref[...], up_ref[at, :] + ub_ref[...]
            sigma = jax.nn.sigmoid(gating)
            dgating = (dhidden * upward * silu_slope(gating, sigma)).astype(BF16)
            dupward = (dhidden * (gating * sigma)).astype(BF16)
            dg_ref[at, :] = dgating
            du_ref[at, :] = dupward
            gsum_ref[...] += jnp.sum(dgating.astype(F32), 0, keepdims=True)
            usum_ref[...] += jnp.sum(dupward.astype(F32), 0, keepdims=True)

    tall = pl.BlockSpec((length, block), lambda j: (0, j))
    flat = pl.BlockSpec((1, block), lambda j: (0, j))
    return pl.pallas_call(
        kernel,
        grid=(steps,),
        in_specs=[
            pl.BlockSpec((length, width), lambda j: (0, 0)),
            pl.BlockSpec((block, width), lambda j: (j, 0)),
            tall,
            pl.BlockSpec((length, block), lambda j: (0, steps + j)),
            flat,
            flat,
        ]
        + [UNREAD] * len(deps),
        out_specs=[tall, tall, flat, flat],
        out_shape=[jax.ShapeDtypeStruct((length, hidden), BF16)] * 2
        + [jax.ShapeDtypeStruct((1, hidden), F32)] * 2,
        scratch_shapes=[pltpu.VMEM((length, block), F32)],
        cost_estimate=COST,
        name="gate_back",
    )(grad, down_full, both, both, gbias[None], ubias[None], *deps)


def mixed_back(dres_low, out_full, retained, swish_pre, ggain, gshift, heads_here, places, deps):
    length, width = dres_low.shape
    value_width = out_full.shape[0]
    block, rows = value_width // heads_here, 128

    size = value_width // places.shape[0]
    chunks = block // size
    aligned = size % 128 == 0

    def kernel(place_ref, d_ref, w_ref, r_ref, s_ref, gain_ref, shift_ref, *rest):
        ds_ref, dr_ref, gsum_ref, ssum_ref, acc_ref, head_ref = rest[len(deps) :]
        if aligned:
            for k in range(chunks):
                at = pl.multiple_of(place_ref[pl.program_id(0) * chunks + k] * size, size)
                head_ref[k * size : (k + 1) * size, :] = w_ref[pl.ds(at, size), :]
            acc_ref[...] = dot(d_ref[...], head_ref[...], NT)
        else:
            acc_ref[...] = dot(d_ref[...], w_ref[...], NT)
        gsum_ref[...] = jnp.zeros_like(gsum_ref)
        ssum_ref[...] = jnp.zeros_like(ssum_ref)

        @pl.loop(0, length // rows)
        def _(i):
            at = pl.ds(pl.multiple_of(i * rows, rows), rows)
            dmixed = acc_ref[at, :]
            normed, factor, active = group_normalize(r_ref[at, :].astype(F32))
            swish = s_ref[at, :]
            sigma = jax.nn.sigmoid(swish)
            dgrouped = dmixed * (swish * sigma)
            grouped = normed * gain_ref[...] + shift_ref[...]
            ds_ref[at, :] = (dmixed * grouped * silu_slope(swish, sigma)).astype(BF16)
            gsum_ref[...] += jnp.sum(dgrouped * normed, 0, keepdims=True)
            ssum_ref[...] += jnp.sum(dgrouped, 0, keepdims=True)
            dr_ref[at, :] = normalize_back(dgrouped * gain_ref[...], normed, factor, active).astype(BF16)

    tall = pl.BlockSpec((length, block), lambda h: (0, h))
    flat = pl.BlockSpec((1, block), lambda h: (0, h))
    return pl.pallas_call(
        kernel,
        grid=(heads_here,),
        in_specs=[
            pl.BlockSpec(memory_space=pltpu.SMEM),
            pl.BlockSpec((length, width), lambda h: (0, 0)),
            pl.BlockSpec((value_width, width), lambda h: (0, 0))
            if aligned
            else pl.BlockSpec((block, width), lambda h: (h, 0)),
            tall,
            tall,
            flat,
            flat,
        ]
        + [UNREAD] * len(deps),
        out_specs=[tall, tall, flat, flat],
        out_shape=[jax.ShapeDtypeStruct((length, value_width), BF16)] * 2
        + [jax.ShapeDtypeStruct((1, value_width), F32)] * 2,
        scratch_shapes=[pltpu.VMEM((length, block), F32), pltpu.VMEM((block, width), BF16)],
        cost_estimate=COST,
        name="mixed_back",
    )(places, dres_low, out_full, retained, swish_pre, ggain[None], gshift[None], *deps)


def full_product(lefts, rights, dims, wide, deps):
    length = lefts[0].shape[0]
    step = min(wide, 512)
    specs = [pl.BlockSpec((length, left.shape[1]), lambda n: (0, 0)) for left in lefts]
    for left, (_, column) in zip(lefts, rights):
        depth = left.shape[1]
        if dims is NT:
            specs.append(pl.BlockSpec((step, depth), lambda n, c=column: (n, c)))
        else:
            specs.append(pl.BlockSpec((depth, step), lambda n: (0, n)))

    def kernel(*refs):
        total = dot(refs[0][...], refs[len(lefts)][...], dims)
        for k in range(1, len(lefts)):
            total += dot(refs[k][...], refs[len(lefts) + k][...], dims)
        refs[-1][...] = total.astype(BF16)

    return pl.pallas_call(
        kernel,
        grid=(wide // step,),
        in_specs=specs + [UNREAD] * len(deps),
        out_specs=pl.BlockSpec((length, step), lambda n: (0, n)),
        out_shape=jax.ShapeDtypeStruct((length, wide), BF16),
        cost_estimate=COST,
        name="full_product",
    )(*lefts, *[right for right, _ in rights], *deps)


class Ring:
    def __init__(self, size):
        half = size // 2
        self.size = size
        self.half = half
        self.order = list(range(half)) + list(range(size - 1, half - 1, -1))
        place = [0] * size
        for position, rank in enumerate(self.order):
            place[rank] = position
        self.right = [(self.order[i], self.order[(i + 1) % size]) for i in range(size)]
        self.left = [(self.order[i], self.order[(i - 1) % size]) for i in range(size)]
        self.me = lax.axis_index("sp")
        self.position = jnp.array(place, jnp.int32)[self.me]

    def rank(self, step):
        return jnp.array(self.order, jnp.int32)[lax.rem(self.position + step + self.size, self.size)]

    def ranks(self, *steps):
        return jnp.stack([self.rank(step) for step in steps])

    def to_right(self, block):
        return lax.ppermute(block, "sp", self.right)

    def to_left(self, block):
        return lax.ppermute(block, "sp", self.left)

    def pieces(self, block):
        middle = block.shape[0] // 2
        found = [(0, block)]
        from_left, from_right = block, block
        for step in range(1, self.half):
            from_left, from_right = self.to_right(from_left), self.to_left(from_right)
            found += [(-step, from_left), (step, from_right)]
        low = self.to_right(from_left[:middle])
        high = self.to_left(from_right[middle:])
        return found, low, high

    def gather(self, block, base=None):
        found, low, high = self.pieces(block)
        if base is None:
            out = jnp.zeros((self.size,) + block.shape, block.dtype)
        else:
            out = after(base, *[part for _, part in found]).reshape((self.size,) + block.shape)
        found.append((self.half, jnp.concatenate([low, high], 0)))
        for step, part in found:
            out = lax.dynamic_update_slice(out, part[None], (self.rank(step), 0, 0))
        return out.reshape(self.size * block.shape[0], block.shape[1])

    def gather_columns(self, pieces, outs, deps):
        found, low, high = pieces
        block = found[0][1]
        rows = block.shape[0]
        widths = [width for width, _ in outs]
        if any(chunk % 128 for _, chunk in outs):
            found.append((self.half, jnp.concatenate([low, high], 0)))
            whole = jnp.zeros((self.size,) + block.shape, block.dtype)
            for step, part in found:
                whole = lax.dynamic_update_slice(whole, part[None], (self.rank(step), 0, 0))
            results, start = [], 0
            for width, chunk in outs:
                share = whole[:, :, start : start + width].reshape(self.size, rows, -1, chunk)
                share = share.transpose(1, 2, 0, 3).reshape(rows, -1)
                results.append(share.astype(F32))
                start += width
            return results
        step_rows = min(64, rows // 2)
        steps = rows // step_rows
        middle = steps // 2
        size = self.size
        ranks = self.ranks(*[step for step, _ in found], self.half)

        def kernel(rank_ref, *refs):
            sources, out_refs = refs[: len(found) + 2], refs[len(found) + 2 + len(deps) :]

            def put(source, rank):
                start = 0
                for (width, chunk), out_ref in zip(outs, out_refs):
                    for k in range(width // chunk):
                        at = pl.multiple_of(k * size * chunk + rank * chunk, 128)
                        piece = source[:, start + k * chunk : start + (k + 1) * chunk]
                        out_ref[:, pl.ds(at, chunk)] = piece.astype(F32)
                    start += width

            for k in range(len(found)):
                put(sources[k], rank_ref[k])

            @pl.when(pl.program_id(0) < middle)
            def _():
                put(sources[-2], rank_ref[len(found)])

            @pl.when(pl.program_id(0) >= middle)
            def _():
                put(sources[-1], rank_ref[len(found)])

        total = block.shape[1]
        in_specs = [pl.BlockSpec((step_rows, total), lambda i, r: (i, 0)) for _ in found]
        in_specs.append(pl.BlockSpec((step_rows, total), lambda i, r: (jnp.minimum(i, middle - 1), 0)))
        in_specs.append(pl.BlockSpec((step_rows, total), lambda i, r: (jnp.maximum(i - middle, 0), 0)))
        return pl.pallas_call(
            kernel,
            grid_spec=pltpu.PrefetchScalarGridSpec(
                num_scalar_prefetch=1,
                grid=(steps,),
                in_specs=in_specs + [UNREAD] * len(deps),
                out_specs=[pl.BlockSpec((step_rows, size * width), lambda i, r: (i, 0)) for width in widths],
            ),
            out_shape=[jax.ShapeDtypeStruct((rows, size * width), F32) for width in widths],
            cost_estimate=COST,
            name="gather_columns",
        )(ranks, *[part for _, part in found], low, high, *deps)

    def gather_rows(self, pieces, deps):
        found, low, high = pieces
        rows, wide = found[0][1].shape
        step = min(wide, 512)
        parts = [part for _, part in found] + [low, high]
        ranks = self.ranks(*[place for place, _ in found], self.half)

        def kernel(rank_ref, *refs):
            out_ref = refs[-1]
            for k in range(len(found) + 2):
                size = parts[k].shape[0]
                at = rank_ref[min(k, len(found))] * rows
                if k == len(found) + 1:
                    at = at + rows - size
                out_ref[pl.ds(pl.multiple_of(at, size), size), :] = refs[k][...].astype(F32)

        return pl.pallas_call(
            kernel,
            grid_spec=pltpu.PrefetchScalarGridSpec(
                num_scalar_prefetch=1,
                grid=(wide // step,),
                in_specs=[pl.BlockSpec((part.shape[0], step), lambda n, r: (0, n)) for part in parts]
                + [UNREAD] * len(deps),
                out_specs=pl.BlockSpec((self.size * rows, step), lambda n, r: (0, n)),
            ),
            out_shape=jax.ShapeDtypeStruct((self.size * rows, wide), F32),
            cost_estimate=COST,
            name="gather_rows",
        )(ranks, *parts, *deps)

    def rows_of(self, terms, step):
        rows = terms.shape[0] // self.size
        return lax.dynamic_slice_in_dim(terms, self.rank(step) * rows, rows, 0)

    def sum_far(self, terms, *others):
        far = self.rows_of(terms, self.half)
        middle = far.shape[0] // 2
        low, high = far[:middle], far[middle:]
        if others:
            low, high = after(low, *others), after(high, *others)
        return (low, high), (self.to_right(low), self.to_left(high))

    def sum_near(self, terms, arrived, *others):
        from_left, from_right = arrived
        for step in range(self.half - 1, 0, -1):
            ahead = self.rows_of(terms, step).astype(F32)
            behind = self.rows_of(terms, -step).astype(F32)
            rows, part = ahead.shape[0], from_left.shape[0]
            ahead = ahead + jnp.pad(from_left.astype(F32), ((0, rows - part), (0, 0)))
            behind = behind + jnp.pad(from_right.astype(F32), ((rows - part, 0), (0, 0)))
            ahead, behind = ahead.astype(BF16), behind.astype(BF16)
            from_left, from_right = self.to_right(ahead), self.to_left(behind)
        return (ahead, behind), (from_left, from_right)

    def sum_own(self, terms, arrived):
        return self.rows_of(terms, 0).astype(F32) + arrived[0].astype(F32) + arrived[1].astype(F32)

    def scatter_sum(self, terms):
        return self.sum_own(terms, self.sum_near(terms, self.sum_far(terms)[1])[1])


class Line:
    def __init__(self, shards):
        self.shards = shards
        self.chips = shards // 2
        index = lax.axis_index("fsdp")
        self.core = lax.rem(index, 2)
        self.groups = [[2 * i + core for i in range(self.chips)] for core in range(2)]
        self.swap = [(i, i ^ 1) for i in range(shards)]

    def to_core(self, block):
        return lax.ppermute(block, "fsdp", self.swap)

    def half(self, left, rights, core, other, deps):
        length = left.shape[0]
        rows = left.shape[1] // self.shards
        wide = sum(right.shape[1] for right in rights)
        if rows % 128:
            columns = [
                lax.dynamic_slice_in_dim(left, (2 * i + core) * rows, rows, 1) for i in range(self.chips)
            ]
            left = after(jnp.concatenate(columns, 1), *deps)
            total = over_rows(left, jnp.concatenate(rights, 1))
            if other is not None:
                total = total + other.astype(F32)
            return total.astype(BF16)
        extra = [] if other is None else [other]

        def kernel(core_ref, x_ref, *refs):
            out_ref = refs[-1]
            start = 0
            for ref, right in zip(refs, rights):
                size = right.shape[1]
                total = dot(x_ref[...], ref[...], TN)
                if extra:
                    total += refs[len(rights)][:, start : start + size].astype(F32)
                out_ref[:, start : start + size] = total.astype(BF16)
                start += size

        return pl.pallas_call(
            kernel,
            grid_spec=pltpu.PrefetchScalarGridSpec(
                num_scalar_prefetch=1,
                grid=(self.chips,),
                in_specs=[pl.BlockSpec((length, rows), lambda i, c: (0, 2 * i + c[0]))]
                + [pl.BlockSpec((length, right.shape[1]), lambda i, c: (0, 0)) for right in rights]
                + [pl.BlockSpec((rows, wide), lambda i, c: (i, 0)) for _ in extra]
                + [UNREAD] * len(deps),
                out_specs=pl.BlockSpec((rows, wide), lambda i, c: (i, 0)),
            ),
            out_shape=jax.ShapeDtypeStruct((self.chips * rows, wide), BF16),
            cost_estimate=COST,
            name="rows_sum",
        )(core.reshape(1), left, *rights, *extra, *deps)

    def theirs(self, left, rights, deps):
        return self.half(left, rights, 1 - self.core, None, deps)

    def mine(self, left, rights, sent, deps):
        return self.half(left, rights, self.core, self.to_core(sent), deps)

    def scatter(self, block):
        return lax.psum_scatter(
            block, "fsdp", scatter_dimension=0, tiled=True, axis_index_groups=self.groups
        )


def butterfly(vector, axes=("fsdp", "sp")):
    for axis in axes:
        size = lax.axis_size(axis)
        step = 1
        while step < size:
            vector = vector + lax.ppermute(vector, axis, [(i, i ^ step) for i in range(size)])
            step *= 2
    return vector


class Spread:
    def __init__(self, shards, parts):
        chips = shards // 2
        assert chips == parts
        if parts == 4:
            moves = [[0, 2, 1, 3], [1, 3, 0, 2], [2, 0, 3, 1], [3, 1, 2, 0]]
        else:
            moves = [[(chip + rank) % chips for chip in range(chips)] for rank in range(parts)]
        self.along, self.across = [], []
        self.places = [[0] * shards for _ in range(parts)]
        self.pieces = [[0] * shards for _ in range(parts)]
        for rank, move in enumerate(moves):
            for chip, target in enumerate(move):
                for core in range(2):
                    middle = (2 * target + core) * parts + rank
                    self.along.append(((2 * chip + core) * parts + rank, middle))
                    self.across.append((middle, (2 * target + core) * parts + chip))
                    piece = core * parts + rank
                    self.places[chip][piece] = 2 * target + core
                    self.pieces[chip][2 * target + core] = piece

    def forth(self, block):
        block = lax.ppermute(block, ("fsdp", "sp"), self.along)
        return lax.ppermute(block, ("fsdp", "sp"), self.across)

    def back(self, block):
        block = lax.ppermute(block, ("fsdp", "sp"), [(there, here) for here, there in self.across])
        return lax.ppermute(block, ("fsdp", "sp"), [(there, here) for here, there in self.along])


def reorder(array, order, size, axis):
    chunks = [
        lax.dynamic_slice_in_dim(array, order[i] * size, size, axis)
        for i in range(array.shape[axis] // size)
    ]
    return jnp.concatenate(chunks, axis)


def local(
    tokens,
    attn_gain,
    attn_shift,
    query_weight,
    key_weight,
    value_weight,
    swish_weight,
    group_gain,
    group_shift,
    out_weight,
    ffn_gain,
    ffn_shift,
    gating_weight,
    upward_weight,
    gating_bias,
    upward_bias,
    downward_weight,
    downward_bias,
    cotangent,
):
    seq_count, local_len, width = tokens.shape
    assert seq_count == 1
    parts = lax.axis_size("sp")
    shards = lax.axis_size("fsdp")
    me = lax.axis_index("sp")
    ring = Ring(parts)
    line = Line(shards)
    heads_here = HEADS // parts
    full_len = local_len * parts
    value_all = value_weight.shape[1]
    hidden_all = gating_weight.shape[1]
    value_width = value_all // parts
    hidden_width = hidden_all // parts
    query_width = query_weight.shape[1] // parts
    third = 2 * query_width + value_width
    chunk = hidden_width // shards

    def columns(weight):
        size = weight.shape[1] // parts
        return lax.dynamic_slice_in_dim(weight, me * size, size, 1)

    def units(weight):
        pieces = [
            lax.dynamic_slice_in_dim(weight, (i * parts + me) * chunk, chunk, weight.ndim - 1)
            for i in range(shards)
        ]
        return jnp.concatenate(pieces, -1)

    def gathered(array):
        return lax.all_gather(array, "fsdp", axis=0, tiled=True)

    small = [
        attn_gain, attn_shift, group_gain, group_shift, ffn_gain, ffn_shift,
        gating_bias, upward_bias, downward_bias,
    ]
    sizes = [item.shape[0] for item in small]
    stacked = jnp.zeros((shards, sum(sizes)), BF16)
    stacked = lax.dynamic_update_slice(
        stacked, jnp.concatenate(small, 0)[None], (lax.axis_index("fsdp"), 0)
    )
    stacked = butterfly(stacked, ("fsdp",))
    offsets = [sum(sizes[:i]) for i in range(len(sizes))]
    (
        gain_one, shift_one, ggain_all, gshift_all, gain_two, shift_two, gbias_all, ubias_all, dbias,
    ) = (
        stacked[:, start : start + size].reshape(-1).astype(F32)
        for start, size in zip(offsets, sizes)
    )
    ggain = lax.dynamic_slice_in_dim(ggain_all, me * value_width, value_width, 0)
    gshift = lax.dynamic_slice_in_dim(gshift_all, me * value_width, value_width, 0)
    gbias = units(gbias_all)
    ubias = units(ubias_all)

    tokens_all = ring.gather(tokens.reshape(-1, width))
    flat = tokens.reshape(-1, width).astype(F32)
    first_norm, first_factor = normalize(flat)
    first = normalize(tokens_all.astype(F32))[0]
    first = (first * gain_one + shift_one).astype(BF16)
    grad_own = cotangent.reshape(-1, width)
    grad_low = ring.gather(after(grad_own, first))

    first_full = gathered(
        jnp.concatenate(
            [columns(query_weight), columns(key_weight), columns(value_weight), columns(swish_weight)], 1
        )
    )
    spread = Spread(shards, parts)
    places = jnp.array(spread.places, jnp.int32)[me]
    rows = out_weight.shape[0] // parts
    out_piece = spread.forth(lax.dynamic_slice_in_dim(out_weight, me * rows, rows, 0))
    out_full = gathered(after(out_piece, first))
    both_full = gathered(jnp.concatenate([units(gating_weight), units(upward_weight)], 1))
    down_full = gathered(lax.dynamic_slice_in_dim(downward_weight, me * rows, rows, 0))

    qkv, swish_pre = project(first, first_full, third)
    rates = decay_rates(me * heads_here + jnp.arange(heads_here))
    retained, mixed = retain_mix(qkv, swish_pre, rates, ggain, gshift, query_width, value_width, places)
    out_ordered = out_full
    if rows % 128:
        mixed = reorder(mixed, jnp.array(spread.pieces, jnp.int32)[me], rows, 1)
        out_ordered = reorder(out_full, places, rows, 0)
    mixed = after(mixed, grad_low)

    terms = full_product([mixed], [(out_full, 0)], NN, width, ())
    resid = flat + ring.scatter_sum(terms)
    spare = terms
    second_norm, second_factor = normalize(resid)
    second = ring.gather((second_norm * gain_two + shift_two).astype(BF16), tokens_all)
    both = product(second, both_full)
    hidden = (jax.nn.silu(both[:, :hidden_width] + gbias) * (both[:, hidden_width:] + ubias)).astype(BF16)

    sent = line.theirs(hidden, [grad_low], ())
    down_sum = line.mine(hidden, [grad_low], sent, ())
    down_share = line.scatter(down_sum)
    dgating, dupward, gbias_term, ubias_term = gate_back(
        grad_low, down_full, both, gbias, ubias, (down_sum,)
    )
    terms = full_product([dgating, dupward], [(both_full, 0), (both_full, 1)], NT, width, ())
    far, arrived = ring.sum_far(terms)
    sent = line.theirs(second, [dgating, dupward], far)
    arrived = lax.optimization_barrier(arrived + (down_share,))[:2]
    near, arrived = ring.sum_near(terms, arrived)
    both_sum = line.mine(second, [dgating, dupward], sent, near)
    both_share = line.scatter(both_sum)
    result = full_product([hidden], [(down_full, 0)], NN, width, (both_sum,))
    dsecond = ring.sum_own(after(terms, result), arrived)
    fgain_term = jnp.sum(dsecond * second_norm, 0)
    fshift_term = jnp.sum(dsecond, 0)
    grad_out = grad_own.astype(F32)
    dbias_term = jnp.sum(grad_out, 0)
    dresid = grad_out + normalize_back(dsecond * gain_two, second_norm, second_factor)

    dres_own = dresid.astype(BF16)
    dres_low = ring.gather(dres_own, spare)
    sent = line.theirs(mixed, [dres_low], ())
    far, result_far = ring.sum_far(result, dres_low)
    out_sum = line.mine(mixed, [dres_low], sent, far)
    out_share = line.scatter(out_sum)
    both_pieces = ring.pieces(after(both_share, out_sum))
    both_near = tuple(part for _, part in both_pieces[0])
    dswish, dretained, ggain_term, gshift_term = mixed_back(
        dres_low, out_ordered, retained, swish_pre, ggain, gshift, heads_here, places, (out_sum, both_share)
    )
    dquery, dkey, dvalue = retain_back(qkv, dretained, rates, query_width, value_width, ())
    sent = line.theirs(first, [dvalue, dswish], both_near + result_far)
    result_far = lax.optimization_barrier(result_far + (sent,))[:2]
    near, result_near = ring.sum_near(result, result_far)
    vs_sum = line.mine(first, [dvalue, dswish], sent, near + (out_share,) + both_pieces[1:])
    vs_share = line.scatter(vs_sum)
    down_pieces = ring.pieces(after(down_share, vs_sum))
    down_near = tuple(part for _, part in down_pieces[0])
    rights = [(first_full, 0), (first_full, 1), (first_full, 2 * query_width // value_width)]
    rights.append((first_full, third // value_width))
    terms = full_product([dquery, dkey, dvalue, dswish], rights, NT, width, (vs_sum,))
    far, arrived = ring.sum_far(after(terms, *(result_near + down_near)))
    sent_qk = line.theirs(first, [dquery, dkey], far)
    arrived = lax.optimization_barrier(arrived + down_pieces[1:])[:2]
    near, arrived = ring.sum_near(terms, arrived)
    qk_sum = line.mine(first, [dquery, dkey], sent_qk, near)
    qk_share = line.scatter(qk_sum)
    result = ring.sum_own(after(result, qk_sum), result_near)
    layer_out = (resid + result + dbias).astype(BF16)
    gating_grad, upward_grad = ring.gather_columns(
        both_pieces, [(hidden_width, chunk), (hidden_width, chunk)], (layer_out,)
    )
    downward_grad = ring.gather_rows(down_pieces, (gating_grad,))
    arrived = lax.optimization_barrier(arrived + (downward_grad,))[:2]
    dfirst = ring.sum_own(terms, arrived)
    again_term = jnp.sum(dfirst * first_norm, 0)
    ashift_term = jnp.sum(dfirst, 0)
    input_grad = dresid + normalize_back(dfirst * gain_one, first_norm, first_factor)

    vs_pieces = ring.pieces(after(vs_share, dfirst))
    vs_near = tuple(part for _, part in vs_pieces[0])
    out_share = spread.back(after(out_share, qk_sum))
    out_pieces = ring.pieces(after(out_share, *vs_near))
    out_grad = ring.gather_rows(out_pieces, ())
    value_grad, swish_grad = ring.gather_columns(
        vs_pieces, [(value_width, value_width), (value_width, value_width)], ()
    )
    query_grad, key_grad = ring.gather_columns(
        ring.pieces(qk_share), [(query_width, query_width), (query_width, query_width)], (value_grad,)
    )

    def placed(term, whole):
        return lax.dynamic_update_slice(jnp.zeros((whole,), F32), term, (me * term.shape[0],))

    def placed_units(term):
        blank = jnp.zeros((shards, parts, chunk), F32)
        return lax.dynamic_update_slice(blank, term.reshape(shards, 1, chunk), (0, me, 0)).reshape(-1)

    terms = [
        again_term, ashift_term, placed(ggain_term[0], value_all), placed(gshift_term[0], value_all),
        fgain_term, fshift_term, placed_units(gbias_term[0]), placed_units(ubias_term[0]), dbias_term,
    ]
    terms = jnp.concatenate([term.reshape(shards, -1) for term in terms], 1)
    totals = butterfly(after(butterfly(after(terms, *vs_near), ("fsdp",)), qk_share), ("sp",))
    mine = lax.dynamic_slice_in_dim(totals, lax.axis_index("fsdp"), 1, 0)[0]
    (
        again_grad, ashift_grad, ggain_grad, gshift_grad, fgain_grad, fshift_grad,
        gbias_grad, ubias_grad, dbias_grad,
    ) = (mine[start : start + size] for start, size in zip(offsets, sizes))
    return (
        layer_out.reshape(seq_count, local_len, width),
        input_grad.reshape(seq_count, local_len, width),
        again_grad,
        ashift_grad,
        query_grad,
        key_grad,
        value_grad,
        swish_grad,
        ggain_grad,
        gshift_grad,
        out_grad,
        fgain_grad,
        fshift_grad,
        gating_grad,
        upward_grad,
        gbias_grad,
        ubias_grad,
        downward_grad,
        dbias_grad,
    )


def solution(mesh):
    row, vector, cube = P("fsdp", None), P("fsdp"), P("fsdp", "sp", None)
    return jax.shard_map(
        local,
        mesh=mesh,
        in_specs=(
            cube, vector, vector, row, row, row, row, vector, vector, row,
            vector, vector, row, row, vector, vector, row, vector, cube,
        ),
        out_specs=(
            cube, cube, vector, vector, row, row, row, row, vector, vector,
            row, vector, vector, row, row, vector, vector, row, vector,
        ),
        check_vma=False,
    )
```

```python
import functools

import jax
import jax.numpy as jnp
from jax import lax
from jax.experimental import pallas as pl
from jax.experimental.pallas import tpu as pltpu
from jax.sharding import PartitionSpec as P

HEADS = 8
EPSILON = 1e-05
BF16 = jnp.bfloat16
F32 = jnp.float32
COST = pl.CostEstimate(flops=1024, bytes_accessed=1024, transcendentals=0)
UNREAD = pl.BlockSpec(memory_space=pl.ANY)
NT = (((1,), (1,)), ((), ()))
NN = (((1,), (0,)), ((), ()))
TN = (((0,), (0,)), ((), ()))


def dot(left, right, dims):
    return lax.dot_general(left, right, dims, preferred_element_type=F32)


def product(left, right):
    return dot(left, right, NN)


def over_rows(left, right):
    return dot(left, right, TN)


def after(value, *others):
    return lax.optimization_barrier((value,) + others)[0]


def normalize(values):
    middle = jnp.mean(values, -1, keepdims=True)
    centred = values - middle
    spread = jnp.mean(centred * centred, -1, keepdims=True)
    factor = lax.rsqrt(spread + EPSILON)
    return (centred * factor, factor)


def group_normalize(values):
    middle = jnp.mean(values, -1, keepdims=True)
    centred = values - middle
    spread = jnp.mean(centred * centred, -1, keepdims=True)
    factor = lax.rsqrt(jnp.maximum(spread, 1.0))
    active = jnp.where(spread > 1.0, 1.0, 0.0)
    return (centred * factor, factor, active)


def normalize_back(scaled, normed, factor, active=1.0):
    first_mean = jnp.mean(scaled, -1, keepdims=True)
    second_mean = jnp.mean(scaled * normed, -1, keepdims=True)
    return factor * (scaled - first_mean - active * normed * second_mean)


def silu_slope(values, sigma):
    return sigma * (1.0 + values * (1.0 - sigma))


def decay_rates(head_ids):
    return jnp.log(1.0 - jnp.exp2(-5.0 - head_ids.astype(F32)))


def decay_block(rate, size, blocks_apart):
    distance = (
        lax.broadcasted_iota(jnp.int32, (size, size), 0)
        - lax.broadcasted_iota(jnp.int32, (size, size), 1)
        + blocks_apart * size
    )
    decay = jnp.exp(jnp.maximum(distance, 0).astype(F32) * rate)
    return jnp.where(distance >= 0, decay, 0.0) if blocks_apart == 0 else decay


def project(first, first_full, third):
    length, width = first.shape
    total = first_full.shape[1]
    step = 512
    steps, low_steps = total // step, third // step

    def kernel(x_ref, w_ref, low_ref, high_ref):
        terms = dot(x_ref[...], w_ref[...], NN)

        @pl.when(pl.program_id(0) < low_steps)
        def _():
            low_ref[...] = terms.astype(BF16)

        @pl.when(pl.program_id(0) >= low_steps)
        def _():
            high_ref[...] = terms

    return pl.pallas_call(
        kernel,
        grid=(steps,),
        in_specs=[
            pl.BlockSpec((length, width), lambda n: (0, 0)),
            pl.BlockSpec((width, step), lambda n: (0, n)),
        ],
        out_specs=[
            pl.BlockSpec((length, step), lambda n: (0, jnp.minimum(n, low_steps - 1))),
            pl.BlockSpec((length, step), lambda n: (0, jnp.maximum(n - low_steps, 0))),
        ],
        out_shape=[
            jax.ShapeDtypeStruct((length, third), BF16),
            jax.ShapeDtypeStruct((length, total - third), F32),
        ],
        cost_estimate=COST,
        name="project",
    )(first, first_full)


def retain_mix(qkv, swish_pre, rates, ggain, gshift, query_width, value_width, places):
    length = qkv.shape[0]
    heads_here = rates.shape[0]
    narrow, wide = query_width // heads_here, value_width // heads_here
    block = 256
    count = length // block
    factor = narrow ** (-0.5)

    size = value_width // places.shape[0]
    chunks = wide // size

    def kernel(rate_ref, place_ref, q_ref, k_ref, v_ref, s_ref, gain_ref, shift_ref, r_ref, m_ref):
        rate = rate_ref[pl.program_id(0)]
        decays = [decay_block(rate, block, apart) for apart in range(count)]
        for i in range(count):
            rows = slice(i * block, (i + 1) * block)
            query = q_ref[rows, :]
            total = jnp.zeros((block, wide), F32)
            for j in range(i + 1):
                cols = slice(j * block, (j + 1) * block)
                weights = (dot(query, k_ref[cols, :], NT) * factor * decays[i - j]).astype(BF16)
                total += dot(weights, v_ref[cols, :], NN)
            retained = total.astype(BF16)
            r_ref[rows, :] = retained
            normed = group_normalize(retained.astype(F32))[0]
            swish = s_ref[rows, :]
            grouped = normed * gain_ref[...] + shift_ref[...]
            mixed = (grouped * (swish * jax.nn.sigmoid(swish))).astype(BF16)
            if size % 128:
                m_ref[rows, :] = mixed
            else:
                for k in range(chunks):
                    at = pl.multiple_of(place_ref[pl.program_id(0) * chunks + k] * size, size)
                    m_ref[rows, pl.ds(at, size)] = mixed[:, k * size : (k + 1) * size]

    def head(width, start):
        return pl.BlockSpec((length, width), lambda h: (0, start // width + h))

    flat = pl.BlockSpec((1, wide), lambda h: (0, h))
    moved = head(wide, 0) if size % 128 else pl.BlockSpec((length, value_width), lambda h: (0, 0))
    return pl.pallas_call(
        kernel,
        grid=(heads_here,),
        in_specs=[
            pl.BlockSpec(memory_space=pltpu.SMEM),
            pl.BlockSpec(memory_space=pltpu.SMEM),
            head(narrow, 0),
            head(narrow, query_width),
            head(wide, 2 * query_width),
            head(wide, 0),
            flat,
            flat,
        ],
        out_specs=[head(wide, 0), moved],
        out_shape=[jax.ShapeDtypeStruct((length, value_width), BF16)] * 2,
        cost_estimate=COST,
        name="retain_mix",
    )(rates, places, qkv, qkv, qkv, swish_pre, ggain[None], gshift[None])


def retain_back(qkv, dretained, rates, query_width, value_width, deps):
    length = qkv.shape[0]
    heads_here = rates.shape[0]
    narrow, wide = query_width // heads_here, value_width // heads_here
    block = 256
    count = length // block
    factor = narrow ** (-0.5)

    def kernel(rate_ref, q_ref, k_ref, v_ref, g_ref, *rest):
        dq_ref, dk_ref, dv_ref, acc_ref = rest[len(deps) :]
        rate = rate_ref[pl.program_id(0)]
        decays = [decay_block(rate, block, apart) for apart in range(count)]
        acc_ref[...] = jnp.zeros_like(acc_ref)
        for j in range(count):
            cols = slice(j * block, (j + 1) * block)
            key, value = k_ref[cols, :], v_ref[cols, :]
            dkey = jnp.zeros((block, narrow), F32)
            dvalue = jnp.zeros((block, wide), F32)
            for i in range(j, count):
                rows = slice(i * block, (i + 1) * block)
                query, grad = q_ref[rows, :], g_ref[rows, :]
                decay = decays[i - j]
                weights = (dot(query, key, NT) * factor * decay).astype(BF16)
                dvalue += dot(weights, grad, TN)
                dscores = (dot(grad, value, NT) * decay).astype(BF16)
                acc_ref[rows, :] += dot(dscores, key, NN)
                dkey += dot(dscores, query, TN)
            dk_ref[cols, :] = (dkey * factor).astype(BF16)
            dv_ref[cols, :] = dvalue.astype(BF16)
        dq_ref[...] = (acc_ref[...] * factor).astype(BF16)

    def head(width, start):
        return pl.BlockSpec((length, width), lambda h: (0, start // width + h))

    return pl.pallas_call(
        kernel,
        grid=(heads_here,),
        in_specs=[
            pl.BlockSpec(memory_space=pltpu.SMEM),
            head(narrow, 0),
            head(narrow, query_width),
            head(wide, 2 * query_width),
            head(wide, 0),
        ]
        + [UNREAD] * len(deps),
        out_specs=[head(narrow, 0), head(narrow, 0), head(wide, 0)],
        out_shape=[
            jax.ShapeDtypeStruct((length, query_width), BF16),
            jax.ShapeDtypeStruct((length, query_width), BF16),
            jax.ShapeDtypeStruct((length, value_width), BF16),
        ],
        scratch_shapes=[pltpu.VMEM((length, narrow), F32)],
        cost_estimate=COST,
        name="retain_back",
    )(rates, qkv, qkv, qkv, dretained, *deps)


def gate_back(grad, down_full, both, gbias, ubias, deps):
    length, width = grad.shape
    hidden = down_full.shape[0]
    block, rows = 256, 128
    steps = hidden // block

    def kernel(g_ref, w_ref, gate_ref, up_ref, gb_ref, ub_ref, *rest):
        dg_ref, du_ref, gsum_ref, usum_ref, acc_ref = rest[len(deps) :]
        acc_ref[...] = dot(g_ref[...], w_ref[...], NT)
        gsum_ref[...] = jnp.zeros_like(gsum_ref)
        usum_ref[...] = jnp.zeros_like(usum_ref)

        @pl.loop(0, length // rows)
        def _(i):
            at = pl.ds(pl.multiple_of(i * rows, rows), rows)
            dhidden = acc_ref[at, :]
            gating, upward = gate_ref[at, :] + gb_ref[...], up_ref[at, :] + ub_ref[...]
            sigma = jax.nn.sigmoid(gating)
            dgating = (dhidden * upward * silu_slope(gating, sigma)).astype(BF16)
            dupward = (dhidden * (gating * sigma)).astype(BF16)
            dg_ref[at, :] = dgating
            du_ref[at, :] = dupward
            gsum_ref[...] += jnp.sum(dgating.astype(F32), 0, keepdims=True)
            usum_ref[...] += jnp.sum(dupward.astype(F32), 0, keepdims=True)

    tall = pl.BlockSpec((length, block), lambda j: (0, j))
    flat = pl.BlockSpec((1, block), lambda j: (0, j))
    return pl.pallas_call(
        kernel,
        grid=(steps,),
        in_specs=[
            pl.BlockSpec((length, width), lambda j: (0, 0)),
            pl.BlockSpec((block, width), lambda j: (j, 0)),
            tall,
            pl.BlockSpec((length, block), lambda j: (0, steps + j)),
            flat,
            flat,
        ]
        + [UNREAD] * len(deps),
        out_specs=[tall, tall, flat, flat],
        out_shape=[jax.ShapeDtypeStruct((length, hidden), BF16)] * 2
        + [jax.ShapeDtypeStruct((1, hidden), F32)] * 2,
        scratch_shapes=[pltpu.VMEM((length, block), F32)],
        cost_estimate=COST,
        name="gate_back",
    )(grad, down_full, both, both, gbias[None], ubias[None], *deps)


def mixed_back(dres_low, out_full, retained, swish_pre, ggain, gshift, heads_here, places, deps):
    length, width = dres_low.shape
    value_width = out_full.shape[0]
    block, rows = value_width // heads_here, 128

    size = value_width // places.shape[0]
    chunks = block // size
    aligned = size % 128 == 0

    def kernel(place_ref, d_ref, w_ref, r_ref, s_ref, gain_ref, shift_ref, *rest):
        ds_ref, dr_ref, gsum_ref, ssum_ref, acc_ref, head_ref = rest[len(deps) :]
        if aligned:
            for k in range(chunks):
                at = pl.multiple_of(place_ref[pl.program_id(0) * chunks + k] * size, size)
                head_ref[k * size : (k + 1) * size, :] = w_ref[pl.ds(at, size), :]
            acc_ref[...] = dot(d_ref[...], head_ref[...], NT)
        else:
            acc_ref[...] = dot(d_ref[...], w_ref[...], NT)
        gsum_ref[...] = jnp.zeros_like(gsum_ref)
        ssum_ref[...] = jnp.zeros_like(ssum_ref)

        @pl.loop(0, length // rows)
        def _(i):
            at = pl.ds(pl.multiple_of(i * rows, rows), rows)
            dmixed = acc_ref[at, :]
            normed, factor, active = group_normalize(r_ref[at, :].astype(F32))
            swish = s_ref[at, :]
            sigma = jax.nn.sigmoid(swish)
            dgrouped = dmixed * (swish * sigma)
            grouped = normed * gain_ref[...] + shift_ref[...]
            ds_ref[at, :] = (dmixed * grouped * silu_slope(swish, sigma)).astype(BF16)
            gsum_ref[...] += jnp.sum(dgrouped * normed, 0, keepdims=True)
            ssum_ref[...] += jnp.sum(dgrouped, 0, keepdims=True)
            dr_ref[at, :] = normalize_back(dgrouped * gain_ref[...], normed, factor, active).astype(BF16)

    tall = pl.BlockSpec((length, block), lambda h: (0, h))
    flat = pl.BlockSpec((1, block), lambda h: (0, h))
    return pl.pallas_call(
        kernel,
        grid=(heads_here,),
        in_specs=[
            pl.BlockSpec(memory_space=pltpu.SMEM),
            pl.BlockSpec((length, width), lambda h: (0, 0)),
            pl.BlockSpec((value_width, width), lambda h: (0, 0))
            if aligned
            else pl.BlockSpec((block, width), lambda h: (h, 0)),
            tall,
            tall,
            flat,
            flat,
        ]
        + [UNREAD] * len(deps),
        out_specs=[tall, tall, flat, flat],
        out_shape=[jax.ShapeDtypeStruct((length, value_width), BF16)] * 2
        + [jax.ShapeDtypeStruct((1, value_width), F32)] * 2,
        scratch_shapes=[pltpu.VMEM((length, block), F32), pltpu.VMEM((block, width), BF16)],
        cost_estimate=COST,
        name="mixed_back",
    )(places, dres_low, out_full, retained, swish_pre, ggain[None], gshift[None], *deps)


def full_product(lefts, rights, dims, wide, deps):
    length = lefts[0].shape[0]
    step = min(wide, 1024)
    specs = [pl.BlockSpec((length, left.shape[1]), lambda n: (0, 0)) for left in lefts]
    for left, (_, column) in zip(lefts, rights):
        depth = left.shape[1]
        if dims is NT:
            specs.append(pl.BlockSpec((step, depth), lambda n, c=column: (n, c)))
        else:
            specs.append(pl.BlockSpec((depth, step), lambda n: (0, n)))

    def kernel(*refs):
        total = dot(refs[0][...], refs[len(lefts)][...], dims)
        for k in range(1, len(lefts)):
            total += dot(refs[k][...], refs[len(lefts) + k][...], dims)
        refs[-1][...] = total.astype(BF16)

    return pl.pallas_call(
        kernel,
        grid=(wide // step,),
        in_specs=specs + [UNREAD] * len(deps),
        out_specs=pl.BlockSpec((length, step), lambda n: (0, n)),
        out_shape=jax.ShapeDtypeStruct((length, wide), BF16),
        cost_estimate=COST,
        name="full_product",
    )(*lefts, *[right for right, _ in rights], *deps)


class Ring:
    def __init__(self, size):
        half = size // 2
        self.size = size
        self.half = half
        self.order = list(range(half)) + list(range(size - 1, half - 1, -1))
        place = [0] * size
        for position, rank in enumerate(self.order):
            place[rank] = position
        self.right = [(self.order[i], self.order[(i + 1) % size]) for i in range(size)]
        self.left = [(self.order[i], self.order[(i - 1) % size]) for i in range(size)]
        self.me = lax.axis_index("sp")
        self.position = jnp.array(place, jnp.int32)[self.me]

    def rank(self, step):
        return jnp.array(self.order, jnp.int32)[lax.rem(self.position + step + self.size, self.size)]

    def ranks(self, *steps):
        return jnp.stack([self.rank(step) for step in steps])

    def to_right(self, block):
        return lax.ppermute(block, "sp", self.right)

    def to_left(self, block):
        return lax.ppermute(block, "sp", self.left)

    def pieces(self, block):
        middle = block.shape[0] // 2
        found = [(0, block)]
        from_left, from_right = block, block
        for step in range(1, self.half):
            from_left, from_right = self.to_right(from_left), self.to_left(from_right)
            found += [(-step, from_left), (step, from_right)]
        low = self.to_right(from_left[:middle])
        high = self.to_left(from_right[middle:])
        return found, low, high

    def gather(self, block, base=None):
        found, low, high = self.pieces(block)
        if base is None:
            out = jnp.zeros((self.size,) + block.shape, block.dtype)
        else:
            out = after(base, *[part for _, part in found]).reshape((self.size,) + block.shape)
        found.append((self.half, jnp.concatenate([low, high], 0)))
        for step, part in found:
            out = lax.dynamic_update_slice(out, part[None], (self.rank(step), 0, 0))
        return out.reshape(self.size * block.shape[0], block.shape[1])

    def gather_columns(self, pieces, outs, deps):
        found, low, high = pieces
        block = found[0][1]
        rows = block.shape[0]
        widths = [width for width, _ in outs]
        if any(chunk % 128 for _, chunk in outs):
            found.append((self.half, jnp.concatenate([low, high], 0)))
            whole = jnp.zeros((self.size,) + block.shape, block.dtype)
            for step, part in found:
                whole = lax.dynamic_update_slice(whole, part[None], (self.rank(step), 0, 0))
            results, start = [], 0
            for width, chunk in outs:
                share = whole[:, :, start : start + width].reshape(self.size, rows, -1, chunk)
                share = share.transpose(1, 2, 0, 3).reshape(rows, -1)
                results.append(share.astype(F32))
                start += width
            return results
        step_rows = min(64, rows // 2)
        steps = rows // step_rows
        middle = steps // 2
        size = self.size
        ranks = self.ranks(*[step for step, _ in found], self.half)

        def kernel(rank_ref, *refs):
            sources, out_refs = refs[: len(found) + 2], refs[len(found) + 2 + len(deps) :]

            def put(source, rank):
                start = 0
                for (width, chunk), out_ref in zip(outs, out_refs):
                    for k in range(width // chunk):
                        at = pl.multiple_of(k * size * chunk + rank * chunk, 128)
                        piece = source[:, start + k * chunk : start + (k + 1) * chunk]
                        out_ref[:, pl.ds(at, chunk)] = piece.astype(F32)
                    start += width

            for k in range(len(found)):
                put(sources[k], rank_ref[k])

            @pl.when(pl.program_id(0) < middle)
            def _():
                put(sources[-2], rank_ref[len(found)])

            @pl.when(pl.program_id(0) >= middle)
            def _():
                put(sources[-1], rank_ref[len(found)])

        total = block.shape[1]
        in_specs = [pl.BlockSpec((step_rows, total), lambda i, r: (i, 0)) for _ in found]
        in_specs.append(pl.BlockSpec((step_rows, total), lambda i, r: (jnp.minimum(i, middle - 1), 0)))
        in_specs.append(pl.BlockSpec((step_rows, total), lambda i, r: (jnp.maximum(i - middle, 0), 0)))
        return pl.pallas_call(
            kernel,
            grid_spec=pltpu.PrefetchScalarGridSpec(
                num_scalar_prefetch=1,
                grid=(steps,),
                in_specs=in_specs + [UNREAD] * len(deps),
                out_specs=[pl.BlockSpec((step_rows, size * width), lambda i, r: (i, 0)) for width in widths],
            ),
            out_shape=[jax.ShapeDtypeStruct((rows, size * width), F32) for width in widths],
            cost_estimate=COST,
            name="gather_columns",
        )(ranks, *[part for _, part in found], low, high, *deps)

    def gather_rows(self, pieces, deps):
        found, low, high = pieces
        rows, wide = found[0][1].shape
        step = min(wide, 512)
        parts = [part for _, part in found] + [low, high]
        ranks = self.ranks(*[place for place, _ in found], self.half)

        def kernel(rank_ref, *refs):
            out_ref = refs[-1]
            for k in range(len(found) + 2):
                size = parts[k].shape[0]
                at = rank_ref[min(k, len(found))] * rows
                if k == len(found) + 1:
                    at = at + rows - size
                out_ref[pl.ds(pl.multiple_of(at, size), size), :] = refs[k][...].astype(F32)

        return pl.pallas_call(
            kernel,
            grid_spec=pltpu.PrefetchScalarGridSpec(
                num_scalar_prefetch=1,
                grid=(wide // step,),
                in_specs=[pl.BlockSpec((part.shape[0], step), lambda n, r: (0, n)) for part in parts]
                + [UNREAD] * len(deps),
                out_specs=pl.BlockSpec((self.size * rows, step), lambda n, r: (0, n)),
            ),
            out_shape=jax.ShapeDtypeStruct((self.size * rows, wide), F32),
            cost_estimate=COST,
            name="gather_rows",
        )(ranks, *parts, *deps)

    def rows_of(self, terms, step):
        rows = terms.shape[0] // self.size
        return lax.dynamic_slice_in_dim(terms, self.rank(step) * rows, rows, 0)

    def sum_far(self, terms, *others):
        far = self.rows_of(terms, self.half)
        middle = far.shape[0] // 2
        low, high = far[:middle], far[middle:]
        if others:
            low, high = after(low, *others), after(high, *others)
        return (low, high), (self.to_right(low), self.to_left(high))

    def sum_near(self, terms, arrived, *others):
        from_left, from_right = arrived
        for step in range(self.half - 1, 0, -1):
            ahead = self.rows_of(terms, step).astype(F32)
            behind = self.rows_of(terms, -step).astype(F32)
            rows, part = ahead.shape[0], from_left.shape[0]
            ahead = ahead + jnp.pad(from_left.astype(F32), ((0, rows - part), (0, 0)))
            behind = behind + jnp.pad(from_right.astype(F32), ((rows - part, 0), (0, 0)))
            ahead, behind = ahead.astype(BF16), behind.astype(BF16)
            from_left, from_right = self.to_right(ahead), self.to_left(behind)
        return (ahead, behind), (from_left, from_right)

    def sum_own(self, terms, arrived):
        return self.rows_of(terms, 0).astype(F32) + arrived[0].astype(F32) + arrived[1].astype(F32)

    def scatter_sum(self, terms):
        return self.sum_own(terms, self.sum_near(terms, self.sum_far(terms)[1])[1])


class Line:
    def __init__(self, shards):
        self.shards = shards
        self.chips = shards // 2
        index = lax.axis_index("fsdp")
        self.core = lax.rem(index, 2)
        self.groups = [[2 * i + core for i in range(self.chips)] for core in range(2)]
        self.swap = [(i, i ^ 1) for i in range(shards)]

    def to_core(self, block):
        return lax.ppermute(block, "fsdp", self.swap)

    def half(self, left, rights, core, other, deps):
        length = left.shape[0]
        rows = left.shape[1] // self.shards
        wide = sum(right.shape[1] for right in rights)
        if rows % 128:
            columns = [
                lax.dynamic_slice_in_dim(left, (2 * i + core) * rows, rows, 1) for i in range(self.chips)
            ]
            left = after(jnp.concatenate(columns, 1), *deps)
            total = over_rows(left, jnp.concatenate(rights, 1))
            if other is not None:
                total = total + other.astype(F32)
            return total.astype(BF16)
        extra = [] if other is None else [other]

        def kernel(core_ref, x_ref, *refs):
            out_ref = refs[-1]
            start = 0
            for ref, right in zip(refs, rights):
                size = right.shape[1]
                total = dot(x_ref[...], ref[...], TN)
                if extra:
                    total += refs[len(rights)][:, start : start + size].astype(F32)
                out_ref[:, start : start + size] = total.astype(BF16)
                start += size

        return pl.pallas_call(
            kernel,
            grid_spec=pltpu.PrefetchScalarGridSpec(
                num_scalar_prefetch=1,
                grid=(self.chips,),
                in_specs=[pl.BlockSpec((length, rows), lambda i, c: (0, 2 * i + c[0]))]
                + [pl.BlockSpec((length, right.shape[1]), lambda i, c: (0, 0)) for right in rights]
                + [pl.BlockSpec((rows, wide), lambda i, c: (i, 0)) for _ in extra]
                + [UNREAD] * len(deps),
                out_specs=pl.BlockSpec((rows, wide), lambda i, c: (i, 0)),
            ),
            out_shape=jax.ShapeDtypeStruct((self.chips * rows, wide), BF16),
            cost_estimate=COST,
            name="rows_sum",
        )(core.reshape(1), left, *rights, *extra, *deps)

    def theirs(self, left, rights, deps):
        return self.half(left, rights, 1 - self.core, None, deps)

    def mine(self, left, rights, sent, deps):
        return self.half(left, rights, self.core, self.to_core(sent), deps)

    def scatter(self, block):
        return lax.psum_scatter(
            block, "fsdp", scatter_dimension=0, tiled=True, axis_index_groups=self.groups
        )


def butterfly(vector, axes=("fsdp", "sp")):
    for axis in axes:
        size = lax.axis_size(axis)
        step = 1
        while step < size:
            vector = vector + lax.ppermute(vector, axis, [(i, i ^ step) for i in range(size)])
            step *= 2
    return vector


class Spread:
    def __init__(self, shards, parts):
        chips = shards // 2
        assert chips == parts
        if parts == 4:
            moves = [[0, 2, 1, 3], [1, 3, 0, 2], [2, 0, 3, 1], [3, 1, 2, 0]]
        else:
            moves = [[(chip + rank) % chips for chip in range(chips)] for rank in range(parts)]
        self.along, self.across = [], []
        self.places = [[0] * shards for _ in range(parts)]
        self.pieces = [[0] * shards for _ in range(parts)]
        for rank, move in enumerate(moves):
            for chip, target in enumerate(move):
                for core in range(2):
                    middle = (2 * target + core) * parts + rank
                    self.along.append(((2 * chip + core) * parts + rank, middle))
                    self.across.append((middle, (2 * target + core) * parts + chip))
                    piece = core * parts + rank
                    self.places[chip][piece] = 2 * target + core
                    self.pieces[chip][2 * target + core] = piece

    def forth(self, block):
        block = lax.ppermute(block, ("fsdp", "sp"), self.along)
        return lax.ppermute(block, ("fsdp", "sp"), self.across)

    def back(self, block):
        block = lax.ppermute(block, ("fsdp", "sp"), [(there, here) for here, there in self.across])
        return lax.ppermute(block, ("fsdp", "sp"), [(there, here) for here, there in self.along])


def reorder(array, order, size, axis):
    chunks = [
        lax.dynamic_slice_in_dim(array, order[i] * size, size, axis)
        for i in range(array.shape[axis] // size)
    ]
    return jnp.concatenate(chunks, axis)


def local(
    tokens,
    attn_gain,
    attn_shift,
    query_weight,
    key_weight,
    value_weight,
    swish_weight,
    group_gain,
    group_shift,
    out_weight,
    ffn_gain,
    ffn_shift,
    gating_weight,
    upward_weight,
    gating_bias,
    upward_bias,
    downward_weight,
    downward_bias,
    cotangent,
):
    seq_count, local_len, width = tokens.shape
    assert seq_count == 1
    parts = lax.axis_size("sp")
    shards = lax.axis_size("fsdp")
    me = lax.axis_index("sp")
    ring = Ring(parts)
    line = Line(shards)
    heads_here = HEADS // parts
    full_len = local_len * parts
    value_all = value_weight.shape[1]
    hidden_all = gating_weight.shape[1]
    value_width = value_all // parts
    hidden_width = hidden_all // parts
    query_width = query_weight.shape[1] // parts
    third = 2 * query_width + value_width
    chunk = hidden_width // shards

    def columns(weight):
        size = weight.shape[1] // parts
        return lax.dynamic_slice_in_dim(weight, me * size, size, 1)

    def units(weight):
        pieces = [
            lax.dynamic_slice_in_dim(weight, (i * parts + me) * chunk, chunk, weight.ndim - 1)
            for i in range(shards)
        ]
        return jnp.concatenate(pieces, -1)

    def gathered(array):
        return lax.all_gather(array, "fsdp", axis=0, tiled=True)

    small = [
        attn_gain, attn_shift, group_gain, group_shift, ffn_gain, ffn_shift,
        gating_bias, upward_bias, downward_bias,
    ]
    sizes = [item.shape[0] for item in small]
    stacked = jnp.zeros((shards, sum(sizes)), BF16)
    stacked = lax.dynamic_update_slice(
        stacked, jnp.concatenate(small, 0)[None], (lax.axis_index("fsdp"), 0)
    )
    stacked = butterfly(stacked, ("fsdp",))
    offsets = [sum(sizes[:i]) for i in range(len(sizes))]
    (
        gain_one, shift_one, ggain_all, gshift_all, gain_two, shift_two, gbias_all, ubias_all, dbias,
    ) = (
        stacked[:, start : start + size].reshape(-1).astype(F32)
        for start, size in zip(offsets, sizes)
    )
    ggain = lax.dynamic_slice_in_dim(ggain_all, me * value_width, value_width, 0)
    gshift = lax.dynamic_slice_in_dim(gshift_all, me * value_width, value_width, 0)
    gbias = units(gbias_all)
    ubias = units(ubias_all)

    tokens_all = ring.gather(tokens.reshape(-1, width))
    flat = tokens.reshape(-1, width).astype(F32)
    first_norm, first_factor = normalize(flat)
    first = normalize(tokens_all.astype(F32))[0]
    first = (first * gain_one + shift_one).astype(BF16)
    grad_own = cotangent.reshape(-1, width)
    grad_low = ring.gather(after(grad_own, first))

    first_full = gathered(
        jnp.concatenate(
            [columns(query_weight), columns(key_weight), columns(value_weight), columns(swish_weight)], 1
        )
    )
    spread = Spread(shards, parts)
    places = jnp.array(spread.places, jnp.int32)[me]
    rows = out_weight.shape[0] // parts
    out_piece = spread.forth(lax.dynamic_slice_in_dim(out_weight, me * rows, rows, 0))
    out_full = gathered(after(out_piece, first))
    both_full = gathered(jnp.concatenate([units(gating_weight), units(upward_weight)], 1))
    down_full = gathered(lax.dynamic_slice_in_dim(downward_weight, me * rows, rows, 0))

    qkv, swish_pre = project(first, first_full, third)
    rates = decay_rates(me * heads_here + jnp.arange(heads_here))
    retained, mixed = retain_mix(qkv, swish_pre, rates, ggain, gshift, query_width, value_width, places)
    out_ordered = out_full
    if rows % 128:
        mixed = reorder(mixed, jnp.array(spread.pieces, jnp.int32)[me], rows, 1)
        out_ordered = reorder(out_full, places, rows, 0)
    mixed = after(mixed, grad_low)

    terms = full_product([mixed], [(out_full, 0)], NN, width, ())
    resid = flat + ring.scatter_sum(terms)
    spare = terms
    second_norm, second_factor = normalize(resid)
    second = ring.gather((second_norm * gain_two + shift_two).astype(BF16), tokens_all)
    both = product(second, both_full)
    hidden = (jax.nn.silu(both[:, :hidden_width] + gbias) * (both[:, hidden_width:] + ubias)).astype(BF16)

    sent = line.theirs(hidden, [grad_low], ())
    down_sum = line.mine(hidden, [grad_low], sent, ())
    down_share = line.scatter(down_sum)
    dgating, dupward, gbias_term, ubias_term = gate_back(
        grad_low, down_full, both, gbias, ubias, (down_sum,)
    )
    terms = full_product([dgating, dupward], [(both_full, 0), (both_full, 1)], NT, width, ())
    far, arrived = ring.sum_far(terms)
    sent = line.theirs(second, [dgating, dupward], far)
    arrived = lax.optimization_barrier(arrived + (down_share,))[:2]
    near, arrived = ring.sum_near(terms, arrived)
    both_sum = line.mine(second, [dgating, dupward], sent, near)
    both_share = line.scatter(both_sum)
    result = full_product([hidden], [(down_full, 0)], NN, width, (both_sum,))
    dsecond = ring.sum_own(after(terms, result), arrived)
    fgain_term = jnp.sum(dsecond * second_norm, 0)
    fshift_term = jnp.sum(dsecond, 0)
    grad_out = grad_own.astype(F32)
    dbias_term = jnp.sum(grad_out, 0)
    dresid = grad_out + normalize_back(dsecond * gain_two, second_norm, second_factor)

    dres_own = dresid.astype(BF16)
    dres_low = ring.gather(dres_own, spare)
    sent = line.theirs(mixed, [dres_low], ())
    far, result_far = ring.sum_far(result, dres_low)
    out_sum = line.mine(mixed, [dres_low], sent, far)
    out_share = line.scatter(out_sum)
    both_pieces = ring.pieces(after(both_share, out_sum))
    both_near = tuple(part for _, part in both_pieces[0])
    dswish, dretained, ggain_term, gshift_term = mixed_back(
        dres_low, out_ordered, retained, swish_pre, ggain, gshift, heads_here, places, (out_sum, both_share)
    )
    dquery, dkey, dvalue = retain_back(qkv, dretained, rates, query_width, value_width, ())
    sent = line.theirs(first, [dvalue, dswish], both_near + result_far)
    result_far = lax.optimization_barrier(result_far + (sent,))[:2]
    near, result_near = ring.sum_near(result, result_far)
    vs_sum = line.mine(first, [dvalue, dswish], sent, near + (out_share,) + both_pieces[1:])
    vs_share = line.scatter(vs_sum)
    down_pieces = ring.pieces(after(down_share, vs_sum))
    down_near = tuple(part for _, part in down_pieces[0])
    rights = [(first_full, 0), (first_full, 1), (first_full, 2 * query_width // value_width)]
    rights.append((first_full, third // value_width))
    terms = full_product([dquery, dkey, dvalue, dswish], rights, NT, width, (vs_sum,))
    far, arrived = ring.sum_far(after(terms, *(result_near + down_near)))
    sent_qk = line.theirs(first, [dquery, dkey], far)
    arrived = lax.optimization_barrier(arrived + down_pieces[1:])[:2]
    near, arrived = ring.sum_near(terms, arrived)
    qk_sum = line.mine(first, [dquery, dkey], sent_qk, near)
    qk_share = line.scatter(qk_sum)
    result = ring.sum_own(after(result, qk_sum), result_near)
    layer_out = (resid + result + dbias).astype(BF16)
    gating_grad, upward_grad = ring.gather_columns(
        both_pieces, [(hidden_width, chunk), (hidden_width, chunk)], (layer_out,)
    )
    downward_grad = ring.gather_rows(down_pieces, (gating_grad,))
    arrived = lax.optimization_barrier(arrived + (downward_grad,))[:2]
    dfirst = ring.sum_own(terms, arrived)
    again_term = jnp.sum(dfirst * first_norm, 0)
    ashift_term = jnp.sum(dfirst, 0)
    input_grad = dresid + normalize_back(dfirst * gain_one, first_norm, first_factor)

    vs_pieces = ring.pieces(after(vs_share, dfirst))
    vs_near = tuple(part for _, part in vs_pieces[0])
    out_share = spread.back(after(out_share, qk_sum))
    out_pieces = ring.pieces(after(out_share, *vs_near))
    out_grad = ring.gather_rows(out_pieces, ())
    value_grad, swish_grad = ring.gather_columns(
        vs_pieces, [(value_width, value_width), (value_width, value_width)], ()
    )
    query_grad, key_grad = ring.gather_columns(
        ring.pieces(qk_share), [(query_width, query_width), (query_width, query_width)], (value_grad,)
    )

    def placed(term, whole):
        return lax.dynamic_update_slice(jnp.zeros((whole,), F32), term, (me * term.shape[0],))

    def placed_units(term):
        blank = jnp.zeros((shards, parts, chunk), F32)
        return lax.dynamic_update_slice(blank, term.reshape(shards, 1, chunk), (0, me, 0)).reshape(-1)

    terms = [
        again_term, ashift_term, placed(ggain_term[0], value_all), placed(gshift_term[0], value_all),
        fgain_term, fshift_term, placed_units(gbias_term[0]), placed_units(ubias_term[0]), dbias_term,
    ]
    terms = jnp.concatenate([term.reshape(shards, -1) for term in terms], 1)
    totals = butterfly(after(butterfly(after(terms, *vs_near), ("fsdp",)), qk_share), ("sp",))
    mine = lax.dynamic_slice_in_dim(totals, lax.axis_index("fsdp"), 1, 0)[0]
    (
        again_grad, ashift_grad, ggain_grad, gshift_grad, fgain_grad, fshift_grad,
        gbias_grad, ubias_grad, dbias_grad,
    ) = (mine[start : start + size] for start, size in zip(offsets, sizes))
    return (
        layer_out.reshape(seq_count, local_len, width),
        input_grad.reshape(seq_count, local_len, width),
        again_grad,
        ashift_grad,
        query_grad,
        key_grad,
        value_grad,
        swish_grad,
        ggain_grad,
        gshift_grad,
        out_grad,
        fgain_grad,
        fshift_grad,
        gating_grad,
        upward_grad,
        gbias_grad,
        ubias_grad,
        downward_grad,
        dbias_grad,
    )


def solution(mesh):
    row, vector, cube = P("fsdp", None), P("fsdp"), P("fsdp", "sp", None)
    return jax.shard_map(
        local,
        mesh=mesh,
        in_specs=(
            cube, vector, vector, row, row, row, row, vector, vector, row,
            vector, vector, row, row, vector, vector, row, vector, cube,
        ),
        out_specs=(
            cube, cube, vector, vector, row, row, row, row, vector, vector,
            row, vector, vector, row, row, vector, vector, row, vector,
        ),
        check_vma=False,
    )
```
